512 devices in a mesh: branch: 8 (over z), cluster: 64 (over x, y, core).
Axes of the slice: x: 4, y: 8, z: 8, core: 2. Of those that a mesh axis runs over, the one named last changes fastest.
Arguments:
- charges: float32 [8192, 16, 256], P(('branch', 'cluster')), may hold values from -6 to 6
- coords: float32 [8192, 3, 256], P(('branch', 'cluster')), may hold values from -4 to 4
- areas: float32 [8192, 256], P(('branch', 'cluster')), may hold values from 0.1 to 1
- col_basis: float32 [8192, 64, 256], P(('branch', 'cluster')), may hold values from -0.375 to 0.375
- row_basis: float32 [8192, 64, 256], P(('branch', 'cluster')), may hold values from -0.75 to 0.75
- leaf_up: float32 [8192, 64, 64], P(('branch', 'cluster')), may hold values from -0.1875 to 0.1875
- leaf_down: float32 [8192, 64, 64], P(('branch', 'cluster')), may hold values from -0.75 to 0.75
- leaf_coupling: float32 [8192, 4, 64, 64], P(('branch', 'cluster')), may hold values from -0.375 to 0.375
- up_transfer: float32 [8, 6, 2, 64, 64], P('branch'), may hold values from -0.5 to 0.5
- down_transfer: float32 [8, 6, 2, 64, 64], P('branch'), may hold values from -0.75 to 0.75
- sibling_coupling: float32 [8, 6, 2, 64, 64], P('branch'), may hold values from -0.75 to 0.75
- branch_coupling: float32 [8, 7, 64, 64], P('branch'), may hold values from -0.25 to 0.25
- near_list: int32 [8192, 16], P(('branch', 'cluster')), may hold values from 0 to 8191, as said below
- far_list: int32 [8192, 4], P(('branch', 'cluster')), may hold values from 0 to 8191, as said below
Outputs:
- potential: float32 [8192, 16, 256], P(('branch', 'cluster'))
The draws below stay inside these ranges and needn't reach their ends.
Inputs may be any that keep to these rules, and one draw needn't show every extreme that they name: `near_list`: row n names 16 distinct leaves of the same branch, each held by the device of leaf n or by one of its two neighbours along the cluster axis; the first entry is n itself. `far_list`: row n names 4 distinct leaves from the same window of three devices as near_list, none of them in row n of near_list.
All inputs are finite; a program needn't handle non-finite values.
Results may differ from the reference program's by a relative error of at most 0.00022.
Values sent between devices are 32-bit elements; how exact they have to be, the bound alone decides.
A program may use at most 64 MiB of HBM per device.

```python
import math
import jax
import jax.numpy as jnp
from jax import lax

PANELS = 256
RANK = 64
SCEN = 16
LEAVES_DEV = 16
NEAR = 16
FAR = 4
BRANCHES = 8
CLUSTERS = 64
LEVELS = 6
LEAVES = 8192


def partner_lists(key):
    shared = jax.random.fold_in(key, 7)
    leaf_ids = jnp.arange(LEAVES, dtype=jnp.int32)
    device_ids = leaf_ids // LEAVES_DEV
    cluster_pos = device_ids % CLUSTERS
    window = jnp.arange(3 * LEAVES_DEV, dtype=jnp.int32)
    candidates = (device_ids * LEAVES_DEV - LEAVES_DEV)[:, None] + window[None, :]
    neighbour_pos = cluster_pos[:, None] + window[None, :] // LEAVES_DEV - 1
    valid = (neighbour_pos >= 0) & (neighbour_pos < CLUSTERS)
    scores = jax.random.randint(shared, (LEAVES, 3 * LEAVES_DEV), 0, 1 << 20, dtype=jnp.int32) * (4 * LEAVES_DEV) + window[None, :]
    scores = jnp.where(valid, scores, -1)
    own_slot = LEAVES_DEV + leaf_ids % LEAVES_DEV
    scores = jnp.where(window[None, :] == own_slot[:, None], 1 << 30, scores)
    best_scores, order = lax.top_k(scores, NEAR + FAR)
    return jnp.take_along_axis(candidates, order, axis=1).astype(jnp.int32)


def draw_near_list(key, part):
    return partner_lists(key)[:, :NEAR]


def draw_far_list(key, part):
    return partner_lists(key)[:, NEAR:]


def block_levels(own_key, dims, cuts, least, largest):
    loudness, own = 1.0, jax.random.fold_in(own_key, 6)
    for dim, blocks in cuts:
        steps = jnp.exp(jax.random.uniform(jax.random.fold_in(own, dim), (blocks,), jnp.float32, least / len(cuts), largest / len(cuts)))
        loudness = loudness * jnp.repeat(steps, dims[dim] // blocks).reshape([-1 if axis == dim else 1 for axis in range(len(dims))])
    return loudness


def bell_draw(own_key, extent, deviation, bound, pieces=(), kind=jnp.bfloat16):
    result = deviation * jax.random.normal(own_key, extent, jnp.float32)
    if pieces:
        result = result * block_levels(own_key, extent, pieces, -0.22, 0.18)
    return jnp.clip(result, -bound, bound).astype(kind)


def setup_inputs(seed: int = 0) -> dict:
    splits = jax.random.split(jax.random.key(seed), 15)
    return {
        "charges": bell_draw(splits[0], (LEAVES, SCEN, PANELS), 1.0, 6.0, ((0, 512),), jnp.float32),
        "coords": bell_draw(splits[1], (LEAVES, 3, PANELS), 1.0, 4.0, ((0, 512),), jnp.float32),
        "areas": jnp.clip(jnp.exp(math.log(1.0) - 2.3025851 * jax.random.uniform(splits[2], (LEAVES, PANELS), jnp.float32) ** block_levels(splits[2], (LEAVES, PANELS), ((0, 512),), -0.2, 0.2)), 0.1, 1.0),
        "col_basis": bell_draw(splits[3], (LEAVES, RANK, PANELS), PANELS ** -0.5, 0.375, ((0, 512),), jnp.float32),
        "row_basis": bell_draw(splits[4], (LEAVES, RANK, PANELS), RANK ** -0.5, 0.75, ((0, 512),), jnp.float32),
        "leaf_up": bell_draw(splits[5], (LEAVES, RANK, RANK), (RANK * LEAVES_DEV) ** -0.5, 0.1875, ((0, 512),), jnp.float32),
        "leaf_down": bell_draw(splits[6], (LEAVES, RANK, RANK), RANK ** -0.5, 0.75, ((0, 512),), jnp.float32),
        "leaf_coupling": bell_draw(splits[7], (LEAVES, FAR, RANK, RANK), (RANK * FAR) ** -0.5, 0.375, ((0, 512),), jnp.float32),
        "up_transfer": bell_draw(splits[8], (BRANCHES, LEVELS, 2, RANK, RANK), (2 * RANK) ** -0.5, 0.5, ((0, 8),), jnp.float32),
        "down_transfer": bell_draw(splits[9], (BRANCHES, LEVELS, 2, RANK, RANK), RANK ** -0.5, 0.75, ((0, 8),), jnp.float32),
        "sibling_coupling": bell_draw(splits[10], (BRANCHES, LEVELS, 2, RANK, RANK), RANK ** -0.5, 0.75, ((0, 8),), jnp.float32),
        "branch_coupling": bell_draw(splits[11], (BRANCHES, BRANCHES - 1, RANK, RANK), (RANK * (BRANCHES - 1)) ** -0.5, 0.25, ((0, 8),), jnp.float32),
        "near_list": draw_near_list(jax.random.fold_in(splits[14], 71), 0),
        "far_list": draw_far_list(jax.random.fold_in(splits[14], 71), 0),
    }


highest = lax.Precision.HIGHEST
reg_square = 0.01
inv_four_pi = 0.25 / math.pi

def near_group(target_coords, near_ids, charges, coords, areas):
    group_size = target_coords.shape[0]
    running = jnp.zeros((group_size, SCEN, PANELS), jnp.float32)
    for slot_index in range(NEAR):
        column_ids = near_ids[:, slot_index]
        src_charge = charges[column_ids]
        src_coords = coords[column_ids]
        src_area = areas[column_ids]
        dist_square = jnp.zeros((group_size, PANELS, PANELS), jnp.float32)
        for axis_index in range(3):
            offset = target_coords[:, axis_index, :, None] - src_coords[:, axis_index, None, :]
            dist_square = dist_square + offset * offset
        kernel = src_area[:, None, :] * inv_four_pi / jnp.sqrt(dist_square + reg_square)
        running = running + jnp.einsum('lpq,lsq->lsp', kernel, src_charge, precision=highest)
    return running

def reference(charges, coords, areas, col_basis, row_basis, leaf_up, leaf_down, leaf_coupling, up_transfer, down_transfer, sibling_coupling, branch_coupling, near_list, far_list):
    device_count = BRANCHES * CLUSTERS

    def per_group(inputs):
        return near_group(inputs[0], inputs[1], charges, coords, areas)
    near_part = lax.map(per_group, (coords.reshape(device_count, LEAVES_DEV, 3, PANELS), near_list.reshape(device_count, LEAVES_DEV, NEAR)))
    near_part = near_part.reshape(LEAVES, SCEN, PANELS)
    leaf_coef = jnp.einsum('nkp,nsp->nks', col_basis, charges, precision=highest)
    far_coef = leaf_coef[far_list]
    leaf_local = jnp.einsum('njac,njcs->nas', leaf_coupling, far_coef, precision=highest)
    node_coef = jnp.einsum('nac,ncs->nas', leaf_up, leaf_coef, precision=highest)
    node_coef = node_coef.reshape(BRANCHES, CLUSTERS, LEAVES_DEV, RANK, SCEN).sum(axis=2)
    upward = [node_coef]
    current = node_coef
    for level_index in range(LEVELS):
        paired = current.reshape(BRANCHES, -1, 2, RANK, SCEN)
        current = jnp.einsum('bac,bgcs->bgas', up_transfer[:, level_index, 0], paired[:, :, 0], precision=highest) + jnp.einsum('bac,bgcs->bgas', up_transfer[:, level_index, 1], paired[:, :, 1], precision=highest)
        upward.append(current)
    branch_roots = current[:, 0]
    partner_ids = (jnp.arange(BRANCHES)[:, None] + 1 + jnp.arange(BRANCHES - 1)[None, :]) % BRANCHES
    downward = jnp.einsum('biac,bics->bas', branch_coupling, branch_roots[partner_ids], precision=highest)[:, None]
    for level_index in reversed(range(LEVELS)):
        level_coef = upward[level_index]
        node_count = level_coef.shape[1]
        sibling_coef = level_coef.reshape(BRANCHES, node_count // 2, 2, RANK, SCEN)[:, :, ::-1].reshape(BRANCHES, node_count, RANK, SCEN)
        parity = jnp.arange(node_count) % 2
        sib_mats = sibling_coupling[:, level_index][:, parity]
        down_mats = down_transfer[:, level_index][:, parity]
        parent = jnp.repeat(downward, 2, axis=1)
        downward = jnp.einsum('bgac,bgcs->bgas', sib_mats, sibling_coef, precision=highest) + jnp.einsum('bgac,bgcs->bgas', down_mats, parent, precision=highest)
    leaf_parent = jnp.repeat(downward.reshape(BRANCHES * CLUSTERS, RANK, SCEN), LEAVES_DEV, axis=0)
    leaf_total = leaf_local + jnp.einsum('nac,ncs->nas', leaf_down, leaf_parent, precision=highest)
    return jnp.einsum('nkp,nks->nsp', row_basis, leaf_total, precision=highest) + near_part
```

```python
import functools
import math

import jax
import jax.numpy as jnp
from jax import lax
from jax.experimental import pallas as pl
from jax.experimental.pallas import tpu as pltpu
from jax.sharding import PartitionSpec as P

f32, bf16 = jnp.float32, jnp.bfloat16
MESH = pl.DeviceIdType.MESH
reg_square = 0.01
inv_four_pi = 0.25 / math.pi

LEAVES, SCEN, PANELS, RANK = 16, 16, 256, 64
NEAR, FAR, LEVELS = 16, 4, 6
NX, NY, NZ, CLUSTERS = 4, 8, 8, 64
FEATURES = 32
PAIRS = ((0, 0), (0, 1), (1, 0), (0, 2), (2, 0), (1, 1), (1, 2), (2, 1))


def dot(a, b, ca, cb):
    return lax.dot_general(a, b, (((ca,), (cb,)), ((), ())), preferred_element_type=f32)


def halves(x):
    high = x.astype(bf16)
    return high, (x - high.astype(f32)).astype(bf16)


def dot3(a, b, cb=1):
    ah, al = halves(a)
    bh, bl = halves(b)
    return dot(ah, bh, 1, cb) + dot(al, bh, 1, cb) + dot(ah, bl, 1, cb)


def features(point, is_source):
    row = lax.broadcasted_iota(jnp.int32, (FEATURES, PANELS), 0)
    dim = row % 3
    coord_row = row < 24
    x, y, z = (jnp.broadcast_to(point[i : i + 1], (FEATURES, PANELS)) for i in range(3))
    square = x * x + y * y + z * z
    value = jnp.where(dim == 0, x, jnp.where(dim == 1, y, z))
    pair = row // 3
    part = jnp.zeros_like(row)
    side = 0 if is_source else 1
    for index, parts in enumerate(PAIRS):
        if parts[side]:
            part = jnp.where(pair == index, parts[side], part)
    if is_source:
        value = jnp.where(coord_row, value, jnp.where(pair == 8, square, 1.0))
        part = jnp.where(pair == 8, dim, part)
    else:
        value = jnp.where(coord_row, -2.0 * value, jnp.where(pair == 8, 1.0, square + reg_square))
        part = jnp.where(pair == 9, dim, part)
    value = jnp.where(row < 30, value, 0.0)
    high = value.astype(bf16).astype(f32)
    rest = value - high
    middle = rest.astype(bf16).astype(f32)
    low = rest - middle
    return jnp.where(part == 0, high, jnp.where(part == 1, middle, low)).astype(bf16)


def body(
    near,
    far,
    charges_hbm,
    coords_hbm,
    areas_hbm,
    col_hbm,
    row_hbm,
    up_hbm,
    down_hbm,
    coupling_hbm,
    up_tr_hbm,
    down_tr_hbm,
    sibling_hbm,
    branch_hbm,
    out,
    charges,
    coords,
    areas,
    coef,
    col,
    rowb,
    leaf_up,
    leaf_down,
    coupling,
    up_tr,
    down_tr,
    sibling,
    branch,
    source,
    weight,
    target,
    node0,
    partner0,
    ynodes,
    nodes2,
    nodes3,
    xnodes,
    nodes5,
    roots,
    down0,
    local_sem,
    send_sem,
    recv_sem,
):
    b = lax.axis_index("branch")
    c = lax.axis_index("cluster")
    core = c % 2
    y = (c // 2) % NY
    x = c // (2 * NY)
    own = pl.ds(LEAVES, LEAVES)

    loads = []
    for source_ref, target_ref in (
        (charges_hbm, charges.at[own]),
        (col_hbm, col),
        (coords_hbm, coords.at[own]),
        (areas_hbm, areas.at[own]),
        (up_hbm, leaf_up),
        (up_tr_hbm, up_tr),
        (sibling_hbm, sibling),
        (down_tr_hbm, down_tr),
        (branch_hbm, branch),
        (coupling_hbm, coupling),
        (down_hbm, leaf_down),
        (row_hbm, rowb),
    ):
        copy = pltpu.make_async_copy(source_ref, target_ref, local_sem.at[len(loads)])
        copy.start()
        loads.append(copy)

    left = (b, (c + CLUSTERS - 1) % CLUSTERS)
    right = (b, (c + 1) % CLUSTERS)
    partner = (b, c + 1 - 2 * core)
    y_peers = [(b, (x * NY + (y + k) % NY) * 2 + core) for k in range(1, NY)]
    x_peers = [(b, (((x + k) % NX) * NY + y) * 2 + core) for k in range(1, NX)]
    z_peers = [((b + k) % NZ, c) for k in range(1, NZ)]

    barrier = pltpu.get_barrier_semaphore()
    everyone = [left, right] + y_peers + x_peers + z_peers
    for peer in everyone:
        pl.semaphore_signal(barrier, inc=1, device_id=peer, device_id_type=MESH)

    def remote(source_ref, target_ref, index, peer):
        return pltpu.make_async_remote_copy(
            src_ref=source_ref,
            dst_ref=target_ref,
            send_sem=send_sem.at[index],
            recv_sem=recv_sem.at[index],
            device_id=peer,
            device_id_type=MESH,
        )

    low_side, high_side = pl.ds(0, LEAVES), pl.ds(2 * LEAVES, LEAVES)

    def neighbour_copies(ref, index):
        return [
            remote(ref.at[own], ref.at[high_side], index, left),
            remote(ref.at[own], ref.at[low_side], index + 1, right),
        ]

    raw = neighbour_copies(coords, 0) + neighbour_copies(areas, 2) + neighbour_copies(charges, 4)
    coefs = neighbour_copies(coef, 6)
    to_partner = remote(node0, partner0, 8, partner)
    to_y = [remote(ynodes.at[y], ynodes.at[y], 9 + k, peer) for k, peer in enumerate(y_peers)]
    to_x = [remote(xnodes.at[x], xnodes.at[x], 16 + k, peer) for k, peer in enumerate(x_peers)]
    to_z = [remote(roots.at[b], roots.at[b], 19 + k, peer) for k, peer in enumerate(z_peers)]

    loads[0].wait()
    loads[1].wait()

    @pl.loop(0, LEAVES // 4)
    def _(step):
        for inner in range(4):
            n = step * 4 + inner
            coef[LEAVES + n] = dot3(charges[LEAVES + n], col[n])

    for index in (2, 3, 4, 5):
        loads[index].wait()
    pl.semaphore_wait(barrier, len(everyone))
    for copy in raw + coefs:
        copy.start()

    def add_leaf(step, total):
        for inner in range(4):
            n = step * 4 + inner
            total = total + dot3(coef[LEAVES + n], leaf_up[n])
        return total

    node0[...] = lax.fori_loop(0, LEAVES // 4, add_leaf, jnp.zeros((SCEN, RANK), f32))
    to_partner.start()

    total = coords[LEAVES]
    for n in range(1, LEAVES):
        total = total + coords[LEAVES + n]
    centre = jnp.sum(total, axis=1, keepdims=True) * (1.0 / (LEAVES * PANELS))

    def prepare(m):
        source[m] = features(coords[m] - centre, True)
        scaled = charges[m] * (areas[pl.ds(m, 1)] * inv_four_pi)
        high, low = halves(scaled)
        weight[m, 0:SCEN] = high
        weight[m, SCEN : 2 * SCEN] = low

    @pl.loop(0, LEAVES // 2)
    def _(step):
        for inner in range(2):
            n = step * 2 + inner
            prepare(LEAVES + n)
            target[n] = features(coords[LEAVES + n] - centre, False)

    def pair_up(level, left_child, right_child):
        return dot3(left_child, up_tr[level, 0]) + dot3(right_child, up_tr[level, 1])

    def rows(nodes, picks):
        parts = [nodes[SCEN * i : SCEN * i + SCEN] for i in picks]
        return parts[0] if len(parts) == 1 else jnp.concatenate(parts, axis=0)

    to_partner.wait()
    mine, other = node0[...], partner0[...]
    even = core == 0
    ynodes[y] = pair_up(0, jnp.where(even, mine, other), jnp.where(even, other, mine))
    for copy in to_y:
        copy.start()
    for copy in raw:
        copy.wait()

    @pl.loop(0, LEAVES // 2)
    def _(step):
        for inner in range(2):
            n = step * 2 + inner
            prepare(n)
            prepare(2 * LEAVES + n)

    def phase_y():
        for copy in to_y:
            copy.wait()
        level = jnp.concatenate([ynodes[i] for i in range(NY)], axis=0)
        level = pair_up(1, rows(level, (0, 2, 4, 6)), rows(level, (1, 3, 5, 7)))
        for i in range(4):
            nodes2[i] = rows(level, (i,))
        level = pair_up(2, rows(level, (0, 2)), rows(level, (1, 3)))
        for i in range(2):
            nodes3[i] = rows(level, (i,))
        xnodes[x] = pair_up(3, rows(level, (0,)), rows(level, (1,)))
        for copy in to_x:
            copy.start()

    def phase_x():
        for copy in to_x:
            copy.wait()
        level = jnp.concatenate([xnodes[i] for i in range(NX)], axis=0)
        level = pair_up(4, rows(level, (0, 2)), rows(level, (1, 3)))
        for i in range(2):
            nodes5[i] = rows(level, (i,))
        roots[b] = pair_up(5, rows(level, (0,)), rows(level, (1,)))
        for copy in to_z:
            copy.start()

    def flipped(index):
        return index + 1 - 2 * (index % 2)

    def phase_z():
        siblings = (
            partner0[...],
            ynodes[flipped(y)],
            nodes2[flipped(y // 2)],
            nodes3[flipped(y // 4)],
            xnodes[flipped(x)],
            nodes5[flipped(x // 2)],
        )
        sides = (core, y % 2, (y // 2) % 2, y // 4, x % 2, x // 2)
        parts = [dot3(siblings[level], sibling[level, sides[level]]) for level in range(LEVELS)]
        for copy in to_z:
            copy.wait()
        down = jnp.zeros((SCEN, RANK), f32)
        for i in range(NZ - 1):
            down = down + dot3(roots[(b + 1 + i) % NZ], branch[i])
        for level in reversed(range(LEVELS)):
            down = parts[level] + dot3(down, down_tr[level, sides[level]])
        down0[...] = down

    shift = LEAVES - (b * CLUSTERS + c) * LEAVES

    def window_index(leaf):
        return jnp.minimum(jnp.maximum(leaf + shift, 0), 3 * LEAVES - 1)

    @pl.loop(0, LEAVES)
    def _(n):
        tn = target[n]
        high_sum = jnp.zeros((2 * SCEN, PANELS), f32)
        low_sum = jnp.zeros((SCEN, PANELS), f32)
        for slot in range(NEAR):
            m = window_index(near[n, slot])
            kernel = lax.rsqrt(dot(source[m], tn, 0, 0))
            kernel_high, kernel_low = halves(kernel)
            wm = weight[m]
            high_sum = high_sum + dot(wm, kernel_high, 1, 0)
            low_sum = low_sum + dot(wm[:SCEN], kernel_low, 1, 0)
        out[n] = high_sum[:SCEN] + high_sum[SCEN:] + low_sum

        @pl.when(n == 0)
        def _():
            for index in range(6, 12):
                loads[index].wait()
            phase_y()

        @pl.when(n == 2)
        def _():
            phase_x()

        @pl.when(n == 5)
        def _():
            phase_z()

    for copy in coefs:
        copy.wait()

    down = down0[...]

    @pl.loop(0, LEAVES // 2)
    def _(step):
        for inner in range(2):
            n = step * 2 + inner
            total = dot3(down, leaf_down[n])
            for slot in range(FAR):
                total = total + dot3(coef[window_index(far[n, slot])], coupling[n, slot])
            out[n] = out[n] + dot3(total, rowb[n], 0)


def on_device(charges, coords, areas, col, row, up, down, coupling, up_tr, down_tr, sib, branch, near, far):
    window = 3 * LEAVES
    hbm = pl.BlockSpec(memory_space=pl.ANY)
    smem = pl.BlockSpec(memory_space=pltpu.SMEM)
    node = (SCEN, RANK)
    square = (RANK, RANK)
    copies = 26
    return pl.pallas_call(
        body,
        out_shape=jax.ShapeDtypeStruct((LEAVES, SCEN, PANELS), f32),
        in_specs=[smem] * 2 + [hbm] * 12,
        out_specs=pl.BlockSpec(memory_space=pltpu.VMEM),
        scratch_shapes=[
            pltpu.VMEM((window, SCEN, PANELS), f32),
            pltpu.VMEM((window, 3, PANELS), f32),
            pltpu.VMEM((window, PANELS), f32),
            pltpu.VMEM((window,) + node, f32),
            pltpu.VMEM((LEAVES, RANK, PANELS), f32),
            pltpu.VMEM((LEAVES, RANK, PANELS), f32),
            pltpu.VMEM((LEAVES,) + square, f32),
            pltpu.VMEM((LEAVES,) + square, f32),
            pltpu.VMEM((LEAVES, FAR) + square, f32),
            pltpu.VMEM((LEVELS, 2) + square, f32),
            pltpu.VMEM((LEVELS, 2) + square, f32),
            pltpu.VMEM((LEVELS, 2) + square, f32),
            pltpu.VMEM((NZ - 1,) + square, f32),
            pltpu.VMEM((window, FEATURES, PANELS), bf16),
            pltpu.VMEM((window, 2 * SCEN, PANELS), bf16),
            pltpu.VMEM((LEAVES, FEATURES, PANELS), bf16),
            pltpu.VMEM(node, f32),
            pltpu.VMEM(node, f32),
            pltpu.VMEM((NY,) + node, f32),
            pltpu.VMEM((4,) + node, f32),
            pltpu.VMEM((2,) + node, f32),
            pltpu.VMEM((NX,) + node, f32),
            pltpu.VMEM((2,) + node, f32),
            pltpu.VMEM((NZ,) + node, f32),
            pltpu.VMEM(node, f32),
            pltpu.SemaphoreType.DMA((12,)),
            pltpu.SemaphoreType.DMA((copies,)),
            pltpu.SemaphoreType.DMA((copies,)),
        ],
        compiler_params=pltpu.CompilerParams(
            collective_id=0, has_side_effects=True, vmem_limit_bytes=48 << 20
        ),
        name="hmatvec",
    )(near, far, charges, coords, areas, col, row, up, down, coupling, up_tr[0], down_tr[0], sib[0], branch[0])


def solution(mesh):
    leaf = ("branch", "cluster")

    def spec(axis, rank):
        return P(axis, *([None] * (rank - 1)))

    in_specs = (
        spec(leaf, 3),
        spec(leaf, 3),
        spec(leaf, 2),
        spec(leaf, 3),
        spec(leaf, 3),
        spec(leaf, 3),
        spec(leaf, 3),
        spec(leaf, 4),
        spec("branch", 5),
        spec("branch", 5),
        spec("branch", 5),
        spec("branch", 4),
        spec(leaf, 2),
        spec(leaf, 2),
    )
    return jax.shard_map(
        on_device, mesh=mesh, in_specs=in_specs, out_specs=spec(leaf, 3), check_vma=False
    )
```

```python
import functools
import math

import jax
import jax.numpy as jnp
from jax import lax
from jax.experimental import pallas as pl
from jax.experimental.pallas import tpu as pltpu
from jax.sharding import PartitionSpec as P

f32, bf16 = jnp.float32, jnp.bfloat16
MESH = pl.DeviceIdType.MESH
reg_square = 0.01
inv_four_pi = 0.25 / math.pi

LEAVES, SCEN, PANELS, RANK = 16, 16, 256, 64
NEAR, FAR, LEVELS = 16, 4, 6
NX, NY, NZ, CLUSTERS = 4, 8, 8, 64
FEATURES = 32
BARRIER_AT = 5
PAIRS = ((0, 0), (0, 1), (1, 0), (0, 2), (2, 0), (1, 1), (1, 2), (2, 1))


def dot(a, b, ca, cb):
    return lax.dot_general(a, b, (((ca,), (cb,)), ((), ())), preferred_element_type=f32)


def halves(x):
    high = x.astype(bf16)
    return high, (x - high.astype(f32)).astype(bf16)


def split_dot(a, b, ca, cb):
    return dot(a[0], b[0], ca, cb) + dot(a[1], b[0], ca, cb) + dot(a[0], b[1], ca, cb)


def dot3(a, b, cb=1):
    return split_dot(halves(a), halves(b), 1, cb)


def features(x, y, z, is_source):
    row = lax.broadcasted_iota(jnp.int32, (FEATURES, PANELS), 0)
    dim = row % 3
    coord_row = row < 24
    x, y, z = (jnp.broadcast_to(value, (FEATURES, PANELS)) for value in (x, y, z))
    square = x * x + y * y + z * z
    value = jnp.where(dim == 0, x, jnp.where(dim == 1, y, z))
    pair = row // 3
    part = jnp.zeros_like(row)
    side = 0 if is_source else 1
    for index, parts in enumerate(PAIRS):
        if parts[side]:
            part = jnp.where(pair == index, parts[side], part)
    if is_source:
        value = jnp.where(coord_row, value, jnp.where(pair == 8, square, 1.0))
        part = jnp.where(pair == 8, dim, part)
    else:
        value = jnp.where(coord_row, -2.0 * value, jnp.where(pair == 8, 1.0, square + reg_square))
        part = jnp.where(pair == 9, dim, part)
    value = jnp.where(row < 30, value, 0.0)
    high = value.astype(bf16).astype(f32)
    rest = value - high
    middle = rest.astype(bf16).astype(f32)
    low = rest - middle
    return jnp.where(part == 0, high, jnp.where(part == 1, middle, low)).astype(bf16)


def place():
    b = lax.axis_index("branch")
    c = lax.axis_index("cluster")
    return b, c, c % 2, (c // 2) % NY, c // (2 * NY)


def remote(source_ref, target_ref, send_sem, recv_sem, index, peer):
    return pltpu.make_async_remote_copy(
        src_ref=source_ref,
        dst_ref=target_ref,
        send_sem=send_sem.at[index],
        recv_sem=recv_sem.at[index],
        device_id=peer,
        device_id_type=MESH,
    )


def greet(peers):
    barrier = pltpu.get_barrier_semaphore()
    for peer in peers:
        pl.semaphore_signal(barrier, inc=1, device_id=peer, device_id_type=MESH)
    return lambda: pl.semaphore_wait(barrier, len(peers))


def start_loads(pairs, sem):
    copies = [pltpu.make_async_copy(a, b, sem.at[i]) for i, (a, b) in enumerate(pairs)]
    for copy in copies:
        copy.start()
    return copies


def flipped(index):
    return index + 1 - 2 * (index % 2)


def exchange(
    charges_hbm,
    coords_hbm,
    areas_hbm,
    col_hbm,
    up_hbm,
    up_tr_hbm,
    coupling_hbm,
    down_hbm,
    row_hbm,
    sibling_hbm,
    far_hbm,
    source_out,
    weight_out,
    target_out,
    base_out,
    high_out,
    low_out,
    root_out,
    parts_out,
    charges,
    coords,
    areas,
    coef,
    col,
    rowb,
    leaf_up,
    leaf_down,
    coupling,
    up_tr,
    sibling,
    far,
    source,
    weight,
    target,
    base,
    down_high,
    down_low,
    node0,
    partner0,
    ynodes,
    nodes2,
    nodes3,
    xnodes,
    nodes5,
    root,
    parts,
    local_sem,
    out_sem,
    send_sem,
    recv_sem,
):
    b, c, core, y, x = place()
    own = pl.ds(LEAVES, LEAVES)
    low_side, high_side = pl.ds(0, LEAVES), pl.ds(2 * LEAVES, LEAVES)
    left = (b, (c + CLUSTERS - 1) % CLUSTERS)
    right = (b, (c + 1) % CLUSTERS)
    partner = (b, flipped(c))
    y_peers = [(b, (x * NY + (y + k) % NY) * 2 + core) for k in range(1, NY)]
    x_peers = [(b, (((x + k) % NX) * NY + y) * 2 + core) for k in range(1, NX)]
    wait_for_all = greet([left, right] + y_peers + x_peers)

    loads = start_loads(
        (
            (coords_hbm, coords.at[:, own]),
            (areas_hbm, areas.at[own]),
            (charges_hbm, charges.at[own]),
            (col_hbm, col),
            (up_hbm, leaf_up),
            (up_tr_hbm, up_tr),
            (coupling_hbm, coupling),
            (row_hbm, rowb),
            (down_hbm, leaf_down),
            (sibling_hbm, sibling),
            (far_hbm, far),
        ),
        local_sem,
    )

    def send(source_ref, target_ref, index, peer):
        return remote(source_ref, target_ref, send_sem, recv_sem, index, peer)

    def sides(ref, index, lead):
        at = (lambda part: ref.at[:, part]) if lead else (lambda part: ref.at[part])
        return [send(at(own), at(high_side), index, left), send(at(own), at(low_side), index + 1, right)]

    coords_copies = sides(coords, 0, True)
    areas_copies = sides(areas, 2, False)
    charges_copies = sides(charges, 4, False)
    coef_copies = sides(coef, 6, False)
    to_partner = send(node0, partner0, 8, partner)
    to_y = [send(ynodes.at[y], ynodes.at[y], 9 + k, peer) for k, peer in enumerate(y_peers)]
    to_x = [send(xnodes.at[x], xnodes.at[x], 16 + k, peer) for k, peer in enumerate(x_peers)]

    for index in range(3):
        loads[index].wait()
    wait_for_all()
    for copy in coords_copies + areas_copies + charges_copies:
        copy.start()

    loads[3].wait()

    @pl.loop(0, LEAVES // 8)
    def _(step):
        for inner in range(8):
            n = step * 8 + inner
            coef[LEAVES + n] = dot3(charges[LEAVES + n], col[n])

    for copy in coef_copies:
        copy.start()
    loads[4].wait()

    def add_leaf(step, total):
        for inner in range(8):
            n = step * 8 + inner
            total = total + dot3(coef[LEAVES + n], leaf_up[n])
        return total

    node0[...] = lax.fori_loop(0, LEAVES // 8, add_leaf, jnp.zeros((SCEN, RANK), f32))
    to_partner.start()

    centres = []
    for i in range(3):
        mean = jnp.sum(coords[i, LEAVES : 2 * LEAVES], axis=0, keepdims=True)
        centres.append(jnp.sum(mean, axis=1, keepdims=True) * (1.0 / (LEAVES * PANELS)))

    def features_of(m, is_source):
        point = [coords[i, pl.ds(m, 1)] - centres[i] for i in range(3)]
        return features(*point, is_source)

    def weigh(m):
        high, low = halves(charges[m] * (areas[pl.ds(m, 1)] * inv_four_pi))
        weight[m, 0:SCEN] = high
        weight[m, SCEN : 2 * SCEN] = low

    @pl.loop(0, LEAVES // 2)
    def _(step):
        for inner in range(2):
            n = step * 2 + inner
            source[LEAVES + n] = features_of(LEAVES + n, True)
            target[n] = features_of(LEAVES + n, False)
            weigh(LEAVES + n)

    def pair_up(level, left_child, right_child):
        return dot3(left_child, up_tr[level, 0]) + dot3(right_child, up_tr[level, 1])

    def rows(nodes, picks):
        found = [nodes[SCEN * i : SCEN * i + SCEN] for i in picks]
        return found[0] if len(found) == 1 else jnp.concatenate(found, axis=0)

    loads[5].wait()
    to_partner.wait()
    mine, other = node0[...], partner0[...]
    even = core == 0
    ynodes[y] = pair_up(0, jnp.where(even, mine, other), jnp.where(even, other, mine))
    for copy in to_y:
        copy.start()

    for copy in coords_copies:
        copy.wait()

    @pl.loop(0, LEAVES // 2)
    def _(step):
        for inner in range(2):
            n = step * 2 + inner
            source[n] = features_of(n, True)
            source[2 * LEAVES + n] = features_of(2 * LEAVES + n, True)

    stores = [
        pltpu.make_async_copy(ref, hbm, out_sem.at[i])
        for i, (ref, hbm) in enumerate(
            (
                (source, source_out),
                (target, target_out),
                (weight, weight_out),
                (base, base_out),
                (down_high, high_out),
                (down_low, low_out),
                (root, root_out),
                (parts, parts_out),
            )
        )
    ]
    stores[0].start()
    stores[1].start()

    for copy in to_y:
        copy.wait()
    level = jnp.concatenate([ynodes[i] for i in range(NY)], axis=0)
    level = pair_up(1, rows(level, (0, 2, 4, 6)), rows(level, (1, 3, 5, 7)))
    for i in range(4):
        nodes2[i] = rows(level, (i,))
    level = pair_up(2, rows(level, (0, 2)), rows(level, (1, 3)))
    for i in range(2):
        nodes3[i] = rows(level, (i,))
    xnodes[x] = pair_up(3, rows(level, (0,)), rows(level, (1,)))
    for copy in to_x:
        copy.start()

    for copy in areas_copies + charges_copies:
        copy.wait()

    @pl.loop(0, LEAVES // 4)
    def _(step):
        for inner in range(4):
            n = step * 4 + inner
            weigh(n)
            weigh(2 * LEAVES + n)

    stores[2].start()

    for index in range(6, 11):
        loads[index].wait()
    for copy in coef_copies:
        copy.wait()
    shift = LEAVES - (b * CLUSTERS + c) * LEAVES

    @pl.loop(0, LEAVES // 2)
    def _(step):
        for inner in range(2):
            n = step * 2 + inner
            total = jnp.zeros((SCEN, RANK), f32)
            for slot in range(FAR):
                m = jnp.minimum(jnp.maximum(far[slot, n] + shift, 0), 3 * LEAVES - 1)
                total = total + dot3(coef[m], coupling[n, slot])
            row_halves = halves(rowb[n])
            base[n] = split_dot(halves(total), row_halves, 1, 0)
            down_high[n], down_low[n] = halves(split_dot(halves(leaf_down[n]), row_halves, 0, 0))

    for index in range(3, 6):
        stores[index].start()

    for copy in to_x:
        copy.wait()
    level = jnp.concatenate([xnodes[i] for i in range(NX)], axis=0)
    level = pair_up(4, rows(level, (0, 2)), rows(level, (1, 3)))
    for i in range(2):
        nodes5[i] = rows(level, (i,))
    root[...] = pair_up(5, rows(level, (0,)), rows(level, (1,)))
    stores[6].start()
    siblings = (
        partner0[...],
        ynodes[flipped(y)],
        nodes2[flipped(y // 2)],
        nodes3[flipped(y // 4)],
        xnodes[flipped(x)],
        nodes5[flipped(x // 2)],
    )
    for index, side in enumerate((core, y % 2, (y // 2) % 2, y // 4, x % 2, x // 2)):
        parts[index] = dot3(siblings[index], sibling[index, side])
    stores[7].start()
    for copy in stores:
        copy.wait()


def near_field(
    near_hbm,
    source_hbm,
    target_hbm,
    weight_hbm,
    base_hbm,
    high_hbm,
    low_hbm,
    root_hbm,
    parts_hbm,
    down_tr_hbm,
    branch_hbm,
    out,
    near,
    source,
    target,
    weight,
    base,
    down_high,
    down_low,
    roots,
    parts,
    down_tr,
    branch,
    local_sem,
    send_sem,
    recv_sem,
):
    b, c, core, y, x = place()
    z_peers = [((b + k) % NZ, c) for k in range(1, NZ)]
    wait_for_all = greet(z_peers)
    loads = start_loads(
        (
            (near_hbm, near),
            (target_hbm, target),
            (source_hbm, source),
            (weight_hbm, weight),
            (base_hbm, base),
            (root_hbm, roots.at[b]),
            (high_hbm, down_high),
            (low_hbm, down_low),
            (parts_hbm, parts),
            (down_tr_hbm, down_tr),
            (branch_hbm, branch),
        ),
        local_sem,
    )
    to_z = [
        remote(roots.at[b], roots.at[b], send_sem, recv_sem, k, peer) for k, peer in enumerate(z_peers)
    ]
    for index in range(5):
        loads[index].wait()
    shift = LEAVES - (b * CLUSTERS + c) * LEAVES

    @pl.loop(0, LEAVES)
    def _(n):
        tn = target[n]
        high_sum = jnp.zeros((2 * SCEN, PANELS), f32)
        low_sum = jnp.zeros((SCEN, PANELS), f32)
        for slot in range(NEAR):
            m = jnp.minimum(jnp.maximum(near[n, slot] + shift, 0), 3 * LEAVES - 1)
            kernel = lax.rsqrt(dot(source[m], tn, 0, 0))
            kernel_high, kernel_low = halves(kernel)
            wm = weight[m]
            high_sum = high_sum + dot(wm, kernel_high, 1, 0)
            low_sum = low_sum + dot(wm[:SCEN], kernel_low, 1, 0)
        out[n] = base[n] + (high_sum[:SCEN] + high_sum[SCEN:] + low_sum)

        @pl.when(n == BARRIER_AT)
        def _():
            wait_for_all()
            loads[5].wait()
            for copy in to_z:
                copy.start()

    for index in range(6, 11):
        loads[index].wait()
    for copy in to_z:
        copy.wait()
    down = jnp.zeros((SCEN, RANK), f32)
    for i in range(NZ - 1):
        down = down + dot3(roots[(b + 1 + i) % NZ], branch[i])
    side = (core, y % 2, (y // 2) % 2, y // 4, x % 2, x // 2)
    for level in reversed(range(LEVELS)):
        down = parts[level] + dot3(down, down_tr[level, side[level]])
    halved = halves(down)

    @pl.loop(0, LEAVES // 8)
    def _(step):
        for inner in range(8):
            n = step * 8 + inner
            out[n] = out[n] + split_dot(halved, (down_high[n], down_low[n]), 1, 0)


def on_device(charges, coords, areas, col, row, up, down, coupling, up_tr, down_tr, sib, branch, near, far):
    window = 3 * LEAVES
    hbm = pl.BlockSpec(memory_space=pltpu.HBM)
    node = (SCEN, RANK)
    square = (RANK, RANK)
    features_shape = (window, FEATURES, PANELS)
    weight_shape = (window, 2 * SCEN, PANELS)
    target_shape = (LEAVES, FEATURES, PANELS)
    leaf_shape = (LEAVES, SCEN, PANELS)
    down_shape = (LEAVES, RANK, PANELS)
    made = (
        (features_shape, bf16),
        (weight_shape, bf16),
        (target_shape, bf16),
        (leaf_shape, f32),
        (down_shape, bf16),
        (down_shape, bf16),
        (node, f32),
        ((LEVELS,) + node, f32),
    )

    def params(collective_id):
        return pltpu.CompilerParams(
            collective_id=collective_id, has_side_effects=True, vmem_limit_bytes=67043328
        )

    scratch = [pltpu.VMEM(shape, kind) for shape, kind in made]
    source, weight, target, base, high, low, root, parts = pl.pallas_call(
        exchange,
        out_shape=[jax.ShapeDtypeStruct(shape, kind) for shape, kind in made],
        in_specs=[hbm] * 11,
        out_specs=[hbm] * 8,
        scratch_shapes=[
            pltpu.VMEM((window, SCEN, PANELS), f32),
            pltpu.VMEM((3, window, PANELS), f32),
            pltpu.VMEM((window, PANELS), f32),
            pltpu.VMEM((window,) + node, f32),
            pltpu.VMEM((LEAVES, RANK, PANELS), f32),
            pltpu.VMEM((LEAVES, RANK, PANELS), f32),
            pltpu.VMEM((LEAVES,) + square, f32),
            pltpu.VMEM((LEAVES,) + square, f32),
            pltpu.VMEM((LEAVES, FAR) + square, f32),
            pltpu.VMEM((LEVELS, 2) + square, f32),
            pltpu.VMEM((LEVELS, 2) + square, f32),
            pltpu.SMEM((FAR, LEAVES), jnp.int32),
        ]
        + scratch[:6]
        + [
            pltpu.VMEM(node, f32),
            pltpu.VMEM(node, f32),
            pltpu.VMEM((NY,) + node, f32),
            pltpu.VMEM((4,) + node, f32),
            pltpu.VMEM((2,) + node, f32),
            pltpu.VMEM((NX,) + node, f32),
            pltpu.VMEM((2,) + node, f32),
        ]
        + scratch[6:]
        + [
            pltpu.SemaphoreType.DMA((11,)),
            pltpu.SemaphoreType.DMA((8,)),
            pltpu.SemaphoreType.DMA((19,)),
            pltpu.SemaphoreType.DMA((19,)),
        ],
        compiler_params=params(0),
        name="exchange",
    )(
        charges,
        jnp.transpose(coords, (1, 0, 2)),
        areas,
        col,
        up,
        up_tr[0],
        coupling,
        down,
        row,
        sib[0],
        far.T,
    )
    return pl.pallas_call(
        near_field,
        out_shape=jax.ShapeDtypeStruct(leaf_shape, f32),
        in_specs=[hbm] * 11,
        out_specs=pl.BlockSpec(memory_space=pltpu.VMEM),
        scratch_shapes=[
            pltpu.SMEM((LEAVES, NEAR), jnp.int32),
            scratch[0],
            scratch[2],
            scratch[1],
            scratch[3],
            scratch[4],
            scratch[5],
            pltpu.VMEM((NZ,) + node, f32),
            scratch[7],
            pltpu.VMEM((LEVELS, 2) + square, f32),
            pltpu.VMEM((NZ - 1,) + square, f32),
            pltpu.SemaphoreType.DMA((11,)),
            pltpu.SemaphoreType.DMA((NZ - 1,)),
            pltpu.SemaphoreType.DMA((NZ - 1,)),
        ],
        compiler_params=params(1),
        name="near_field",
    )(near, source, target, weight, base, high, low, root, parts, down_tr[0], branch[0])


def solution(mesh):
    leaf = ("branch", "cluster")

    def spec(axis, rank):
        return P(axis, *([None] * (rank - 1)))

    in_specs = (
        spec(leaf, 3),
        spec(leaf, 3),
        spec(leaf, 2),
        spec(leaf, 3),
        spec(leaf, 3),
        spec(leaf, 3),
        spec(leaf, 3),
        spec(leaf, 4),
        spec("branch", 5),
        spec("branch", 5),
        spec("branch", 5),
        spec("branch", 4),
        spec(leaf, 2),
        spec(leaf, 2),
    )
    return jax.shard_map(
        on_device, mesh=mesh, in_specs=in_specs, out_specs=spec(leaf, 3), check_vma=False
    )
```

```python
import functools
import math

import jax
import jax.numpy as jnp
from jax import lax
from jax.experimental import pallas as pl
from jax.experimental.pallas import tpu as pltpu
from jax.sharding import PartitionSpec as P

f32, bf16 = jnp.float32, jnp.bfloat16
MESH = pl.DeviceIdType.MESH
reg_square = 0.01
inv_four_pi = 0.25 / math.pi

LEAVES, SCEN, PANELS, RANK = 16, 16, 256, 64
NEAR, FAR, LEVELS = 16, 4, 6
NX, NY, NZ, CLUSTERS = 4, 8, 8, 64
FEATURES = 32
FULL_VMEM = 67043328
BARRIER_AT, Y_AT, X_AT = 3, 6, 8
PAIRS = ((0, 0), (0, 1), (1, 0), (0, 2), (2, 0), (1, 1), (1, 2), (2, 1))


def dot(a, b, ca, cb):
    return lax.dot_general(a, b, (((ca,), (cb,)), ((), ())), preferred_element_type=f32)


def halves(x):
    high = x.astype(bf16)
    return high, (x - high.astype(f32)).astype(bf16)


def split_dot(a, b, ca, cb):
    rows = a[0].shape[1 - ca]
    both = dot(jnp.concatenate(a, axis=1 - ca), b[0], ca, cb)
    return both[:rows] + both[rows:] + dot(a[0], b[1], ca, cb)


def dot3(a, b, cb=1):
    return split_dot(halves(a), halves(b), 1, cb)


def features(x, y, z, is_source):
    row = lax.broadcasted_iota(jnp.int32, (FEATURES, PANELS), 0)
    dim = row % 3
    coord_row = row < 24
    x, y, z = (jnp.broadcast_to(value, (FEATURES, PANELS)) for value in (x, y, z))
    square = x * x + y * y + z * z
    value = jnp.where(dim == 0, x, jnp.where(dim == 1, y, z))
    pair = row // 3
    part = jnp.zeros_like(row)
    side = 0 if is_source else 1
    for index, parts in enumerate(PAIRS):
        if parts[side]:
            part = jnp.where(pair == index, parts[side], part)
    if is_source:
        value = jnp.where(coord_row, value, jnp.where(pair == 8, square, 1.0))
        part = jnp.where(pair == 8, dim, part)
    else:
        value = jnp.where(coord_row, -2.0 * value, jnp.where(pair == 8, 1.0, square + reg_square))
        part = jnp.where(pair == 9, dim, part)
    value = jnp.where(row < 30, value, 0.0)
    high = value.astype(bf16).astype(f32)
    rest = value - high
    middle = rest.astype(bf16).astype(f32)
    low = rest - middle
    return jnp.where(part == 0, high, jnp.where(part == 1, middle, low)).astype(bf16)


def place():
    b = lax.axis_index("branch")
    c = lax.axis_index("cluster")
    return b, c, c % 2, (c // 2) % NY, c // (2 * NY)


def remote(source_ref, target_ref, send_sem, recv_sem, index, peer):
    return pltpu.make_async_remote_copy(
        src_ref=source_ref,
        dst_ref=target_ref,
        send_sem=send_sem.at[index],
        recv_sem=recv_sem.at[index],
        device_id=peer,
        device_id_type=MESH,
    )


def greet(peers):
    barrier = pltpu.get_barrier_semaphore()
    for peer in peers:
        pl.semaphore_signal(barrier, inc=1, device_id=peer, device_id_type=MESH)
    return lambda: pl.semaphore_wait(barrier, len(peers))


def start_loads(pairs, sem):
    copies = [pltpu.make_async_copy(a, b, sem.at[i]) for i, (a, b) in enumerate(pairs)]
    for copy in copies:
        copy.start()
    return copies


def flipped(index):
    return index + 1 - 2 * (index % 2)


def pair_up(up_tr, level, left_child, right_child):
    return dot3(left_child, up_tr[level, 0]) + dot3(right_child, up_tr[level, 1])


def rows(nodes, picks):
    found = [nodes[SCEN * i : SCEN * i + SCEN] for i in picks]
    return found[0] if len(found) == 1 else jnp.concatenate(found, axis=0)


def exchange(
    charges_hbm,
    coords_hbm,
    areas_hbm,
    col_hbm,
    up_hbm,
    up_tr_hbm,
    source_out,
    weight_out,
    target_out,
    coef_out,
    pair_out,
    partner_out,
    charges,
    coords,
    areas,
    col,
    leaf_up,
    up_tr,
    node0,
    source,
    weight,
    target,
    coef,
    pair,
    partner0,
    local_sem,
    out_sem,
    send_sem,
    recv_sem,
):
    b, c, core, y, x = place()
    own = pl.ds(LEAVES, LEAVES)
    low_side, high_side = pl.ds(0, LEAVES), pl.ds(2 * LEAVES, LEAVES)
    left = (b, (c + CLUSTERS - 1) % CLUSTERS)
    right = (b, (c + 1) % CLUSTERS)
    partner = (b, flipped(c))
    wait_for_all = greet([left, right])

    loads = start_loads(
        (
            (coords_hbm, coords.at[:, own]),
            (areas_hbm, areas.at[own]),
            (charges_hbm, charges.at[own]),
            (col_hbm, col),
            (up_hbm, leaf_up),
            (up_tr_hbm, up_tr),
        ),
        local_sem,
    )

    def send(source_ref, target_ref, index, peer):
        return remote(source_ref, target_ref, send_sem, recv_sem, index, peer)

    def sides(ref, index, lead):
        at = (lambda part: ref.at[:, part]) if lead else (lambda part: ref.at[part])
        return [send(at(own), at(high_side), index, left), send(at(own), at(low_side), index + 1, right)]

    coords_copies = sides(coords, 0, True)
    areas_copies = sides(areas, 2, False)
    charges_copies = sides(charges, 4, False)
    coef_copies = sides(coef, 6, False)
    to_partner = send(node0, partner0, 8, partner)

    for index in range(3):
        loads[index].wait()
    wait_for_all()
    for copy in coords_copies + areas_copies + charges_copies:
        copy.start()

    loads[3].wait()

    @pl.loop(0, LEAVES // 8)
    def _(step):
        for inner in range(8):
            n = step * 8 + inner
            coef[LEAVES + n] = dot3(charges[LEAVES + n], col[n])

    for copy in coef_copies:
        copy.start()
    loads[4].wait()

    def add_leaf(step, total):
        for inner in range(8):
            n = step * 8 + inner
            total = total + dot3(coef[LEAVES + n], leaf_up[n])
        return total

    node0[...] = lax.fori_loop(0, LEAVES // 8, add_leaf, jnp.zeros((SCEN, RANK), f32))
    to_partner.start()

    centres = []
    for i in range(3):
        mean = jnp.sum(coords[i, LEAVES : 2 * LEAVES], axis=0, keepdims=True)
        centres.append(jnp.sum(mean, axis=1, keepdims=True) * (1.0 / (LEAVES * PANELS)))

    def features_of(m, is_source):
        point = [coords[i, pl.ds(m, 1)] - centres[i] for i in range(3)]
        return features(*point, is_source)

    def weigh(m):
        high, low = halves(charges[m] * (areas[pl.ds(m, 1)] * inv_four_pi))
        weight[m, 0:SCEN] = high
        weight[m, SCEN : 2 * SCEN] = low

    @pl.loop(0, LEAVES // 2)
    def _(step):
        for inner in range(2):
            n = step * 2 + inner
            source[LEAVES + n] = features_of(LEAVES + n, True)
            target[n] = features_of(LEAVES + n, False)
            weigh(LEAVES + n)

    parts = []

    def store(ref, hbm):
        copy = pltpu.make_async_copy(ref, hbm, out_sem.at[len(parts)])
        copy.start()
        parts.append(copy)

    store(target, target_out)
    store(source.at[own], source_out.at[own])
    store(weight.at[own], weight_out.at[own])

    loads[5].wait()
    to_partner.wait()
    mine, other = node0[...], partner0[...]
    even = core == 0
    pair[...] = pair_up(up_tr, 0, jnp.where(even, mine, other), jnp.where(even, other, mine))
    store(pair, pair_out)
    store(partner0, partner_out)

    for copy in coords_copies:
        copy.wait()

    @pl.loop(0, LEAVES // 2)
    def _(step):
        for inner in range(2):
            n = step * 2 + inner
            source[n] = features_of(n, True)
            source[2 * LEAVES + n] = features_of(2 * LEAVES + n, True)

    store(source.at[low_side], source_out.at[low_side])
    store(source.at[high_side], source_out.at[high_side])
    for copy in areas_copies + charges_copies:
        copy.wait()

    @pl.loop(0, LEAVES // 4)
    def _(step):
        for inner in range(4):
            n = step * 4 + inner
            weigh(n)
            weigh(2 * LEAVES + n)

    store(weight.at[low_side], weight_out.at[low_side])
    store(weight.at[high_side], weight_out.at[high_side])
    for copy in coef_copies:
        copy.wait()
    store(coef, coef_out)
    for copy in parts:
        copy.wait()


def near_field(
    near_hbm,
    far_hbm,
    source_hbm,
    target_hbm,
    weight_hbm,
    coef_hbm,
    pair_hbm,
    partner_hbm,
    coupling_hbm,
    down_hbm,
    row_hbm,
    up_tr_hbm,
    sibling_hbm,
    down_tr_hbm,
    branch_hbm,
    out,
    near,
    far,
    source,
    target,
    weight,
    coef,
    partner0,
    coupling,
    leaf_down,
    rowb,
    up_tr,
    sibling,
    down_tr,
    branch,
    local,
    down_high,
    down_low,
    ynodes,
    nodes2,
    nodes3,
    xnodes,
    nodes5,
    roots,
    local_sem,
    send_sem,
    recv_sem,
):
    b, c, core, y, x = place()
    y_peers = [(b, (x * NY + (y + k) % NY) * 2 + core) for k in range(1, NY)]
    x_peers = [(b, (((x + k) % NX) * NY + y) * 2 + core) for k in range(1, NX)]
    z_peers = [((b + k) % NZ, c) for k in range(1, NZ)]
    wait_for_all = greet(y_peers + x_peers + z_peers)
    loads = start_loads(
        (
            (near_hbm, near),
            (target_hbm, target),
            (source_hbm, source),
            (weight_hbm, weight),
            (pair_hbm, ynodes.at[y]),
            (up_tr_hbm, up_tr),
            (far_hbm, far),
            (coef_hbm, coef),
            (coupling_hbm, coupling),
            (row_hbm, rowb),
            (down_hbm, leaf_down),
            (partner_hbm, partner0),
            (sibling_hbm, sibling),
            (down_tr_hbm, down_tr),
            (branch_hbm, branch),
        ),
        local_sem,
    )

    def send(source_ref, target_ref, index, peer):
        return remote(source_ref, target_ref, send_sem, recv_sem, index, peer)

    to_y = [send(ynodes.at[y], ynodes.at[y], k, peer) for k, peer in enumerate(y_peers)]
    to_x = [send(xnodes.at[x], xnodes.at[x], 7 + k, peer) for k, peer in enumerate(x_peers)]
    to_z = [send(roots.at[b], roots.at[b], 10 + k, peer) for k, peer in enumerate(z_peers)]
    for index in range(4):
        loads[index].wait()
    shift = LEAVES - (b * CLUSTERS + c) * LEAVES

    def window_index(leaf):
        return jnp.minimum(jnp.maximum(leaf + shift, 0), 3 * LEAVES - 1)

    @pl.loop(0, LEAVES)
    def _(n):
        tn = target[n]
        high_sum = jnp.zeros((2 * SCEN, PANELS), f32)
        low_sum = jnp.zeros((SCEN, PANELS), f32)
        for slot in range(NEAR):
            m = window_index(near[n, slot])
            kernel = lax.rsqrt(dot(source[m], tn, 0, 0))
            kernel_high, kernel_low = halves(kernel)
            wm = weight[m]
            high_sum = high_sum + dot(wm, kernel_high, 1, 0)
            low_sum = low_sum + dot(wm[:SCEN], kernel_low, 1, 0)
        out[n] = high_sum[:SCEN] + high_sum[SCEN:] + low_sum

        @pl.when(n == BARRIER_AT)
        def _():
            loads[4].wait()
            loads[5].wait()
            wait_for_all()
            for copy in to_y:
                copy.start()

        @pl.when(n == Y_AT)
        def _():
            for copy in to_y:
                copy.wait()
            level = jnp.concatenate([ynodes[i] for i in range(NY)], axis=0)
            level = pair_up(up_tr, 1, rows(level, (0, 2, 4, 6)), rows(level, (1, 3, 5, 7)))
            for i in range(4):
                nodes2[i] = rows(level, (i,))
            level = pair_up(up_tr, 2, rows(level, (0, 2)), rows(level, (1, 3)))
            for i in range(2):
                nodes3[i] = rows(level, (i,))
            xnodes[x] = pair_up(up_tr, 3, rows(level, (0,)), rows(level, (1,)))
            for copy in to_x:
                copy.start()

        @pl.when(n == X_AT)
        def _():
            for copy in to_x:
                copy.wait()
            level = jnp.concatenate([xnodes[i] for i in range(NX)], axis=0)
            level = pair_up(up_tr, 4, rows(level, (0, 2)), rows(level, (1, 3)))
            for i in range(2):
                nodes5[i] = rows(level, (i,))
            roots[b] = pair_up(up_tr, 5, rows(level, (0,)), rows(level, (1,)))
            for copy in to_z:
                copy.start()

    for index in range(6, 15):
        loads[index].wait()

    @pl.loop(0, LEAVES // 8)
    def _(step):
        for inner in range(8):
            n = step * 8 + inner
            total = jnp.zeros((SCEN, RANK), f32)
            for slot in range(FAR):
                total = total + dot3(coef[window_index(far[slot, n])], coupling[n, slot])
            local[n] = total

    @pl.loop(0, LEAVES // 4)
    def _(step):
        for inner in range(4):
            n = step * 4 + inner
            row_halves = halves(rowb[n])
            out[n] = out[n] + split_dot(halves(local[n]), row_halves, 1, 0)
            down_high[n], down_low[n] = halves(split_dot(halves(leaf_down[n]), row_halves, 0, 0))

    siblings = (
        partner0[...],
        ynodes[flipped(y)],
        nodes2[flipped(y // 2)],
        nodes3[flipped(y // 4)],
        xnodes[flipped(x)],
        nodes5[flipped(x // 2)],
    )
    side = (core, y % 2, (y // 2) % 2, y // 4, x % 2, x // 2)
    known = jnp.zeros((SCEN, RANK), f32)
    for level in reversed(range(LEVELS)):
        known = dot3(siblings[level], sibling[level, side[level]]) + dot3(known, down_tr[level, side[level]])
    chain = down_tr[0, side[0]]
    for level in range(1, LEVELS):
        chain = dot3(chain, down_tr[level, side[level]], 0)
    chain_halves = halves(chain)
    for copy in to_z:
        copy.wait()
    top = jnp.zeros((SCEN, RANK), f32)
    for i in range(NZ - 1):
        top = top + dot3(roots[(b + 1 + i) % NZ], branch[i])
    halved = halves(known + split_dot(halves(top), chain_halves, 1, 1))

    @pl.loop(0, LEAVES // 8)
    def _(step):
        for inner in range(8):
            n = step * 8 + inner
            out[n] = out[n] + split_dot(halved, (down_high[n], down_low[n]), 1, 0)


def on_device(charges, coords, areas, col, row, up, down, coupling, up_tr, down_tr, sib, branch, near, far):
    window = 3 * LEAVES
    hbm = pl.BlockSpec(memory_space=pltpu.HBM)
    node = (SCEN, RANK)
    square = (RANK, RANK)
    leaf_shape = (LEAVES, SCEN, PANELS)
    down_shape = (LEAVES, RANK, PANELS)
    made = (
        ((window, FEATURES, PANELS), bf16),
        ((window, 2 * SCEN, PANELS), bf16),
        ((LEAVES, FEATURES, PANELS), bf16),
        ((window,) + node, f32),
        (node, f32),
        (node, f32),
    )

    def vmem(*shape):
        return pltpu.VMEM(shape, f32)

    def params(collective_id, limit):
        return pltpu.CompilerParams(
            collective_id=collective_id, has_side_effects=True, vmem_limit_bytes=limit
        )

    scratch = [pltpu.VMEM(shape, kind) for shape, kind in made]
    transfer = vmem(LEVELS, 2, *square)
    source, weight, target, coef, pair, partner = pl.pallas_call(
        exchange,
        out_shape=[jax.ShapeDtypeStruct(shape, kind) for shape, kind in made],
        in_specs=[hbm] * 6,
        out_specs=[hbm] * 6,
        scratch_shapes=[
            vmem(window, SCEN, PANELS),
            vmem(3, window, PANELS),
            vmem(window, PANELS),
            vmem(LEAVES, RANK, PANELS),
            vmem(LEAVES, *square),
            transfer,
            vmem(*node),
        ]
        + scratch
        + [
            pltpu.SemaphoreType.DMA((6,)),
            pltpu.SemaphoreType.DMA((10,)),
            pltpu.SemaphoreType.DMA((9,)),
            pltpu.SemaphoreType.DMA((9,)),
        ],
        compiler_params=params(0, FULL_VMEM),
        name="exchange",
    )(charges, jnp.transpose(coords, (1, 0, 2)), areas, col, up, up_tr[0])
    return pl.pallas_call(
        near_field,
        out_shape=jax.ShapeDtypeStruct(leaf_shape, f32),
        in_specs=[hbm] * 15,
        out_specs=pl.BlockSpec(memory_space=pltpu.VMEM),
        scratch_shapes=[
            pltpu.SMEM((LEAVES, NEAR), jnp.int32),
            pltpu.SMEM((FAR, LEAVES), jnp.int32),
            scratch[0],
            scratch[2],
            scratch[1],
            scratch[3],
            scratch[5],
            vmem(LEAVES, FAR, *square),
            vmem(LEAVES, *square),
            vmem(LEAVES, RANK, PANELS),
            transfer,
            transfer,
            transfer,
            vmem(NZ - 1, *square),
            vmem(LEAVES, *node),
            pltpu.VMEM(down_shape, bf16),
            pltpu.VMEM(down_shape, bf16),
            vmem(NY, *node),
            vmem(4, *node),
            vmem(2, *node),
            vmem(NX, *node),
            vmem(2, *node),
            vmem(NZ, *node),
            pltpu.SemaphoreType.DMA((15,)),
            pltpu.SemaphoreType.DMA((17,)),
            pltpu.SemaphoreType.DMA((17,)),
        ],
        compiler_params=params(1, FULL_VMEM),
        name="near_field",
    )(
        near,
        far.T,
        source,
        target,
        weight,
        coef,
        pair,
        partner,
        coupling,
        down,
        row,
        up_tr[0],
        sib[0],
        down_tr[0],
        branch[0],
    )


def solution(mesh):
    leaf = ("branch", "cluster")

    def spec(axis, rank):
        return P(axis, *([None] * (rank - 1)))

    in_specs = (
        spec(leaf, 3),
        spec(leaf, 3),
        spec(leaf, 2),
        spec(leaf, 3),
        spec(leaf, 3),
        spec(leaf, 3),
        spec(leaf, 3),
        spec(leaf, 4),
        spec("branch", 5),
        spec("branch", 5),
        spec("branch", 5),
        spec("branch", 4),
        spec(leaf, 2),
        spec(leaf, 2),
    )
    return jax.shard_map(
        on_device, mesh=mesh, in_specs=in_specs, out_specs=spec(leaf, 3), check_vma=False
    )
```

```python
import functools
import math

import jax
import jax.numpy as jnp
from jax import lax
from jax.experimental import pallas as pl
from jax.experimental.pallas import tpu as pltpu
from jax.sharding import PartitionSpec as P

f32, bf16 = jnp.float32, jnp.bfloat16
MESH = pl.DeviceIdType.MESH
reg_square = 0.01
inv_four_pi = 0.25 / math.pi

LEAVES, SCEN, PANELS, RANK = 16, 16, 256, 64
NEAR, FAR, LEVELS = 16, 4, 6
NX, NY, NZ, CLUSTERS = 4, 8, 8, 64
FEATURES = 32
FULL_VMEM = 67043328
GROUP = 2
BARRIER_AT, Y_AT, X_AT = 1, 2, 3
PAIRS = ((0, 0), (0, 1), (1, 0), (0, 2), (2, 0), (1, 1), (1, 2), (2, 1))


def dot(a, b, ca, cb):
    return lax.dot_general(a, b, (((ca,), (cb,)), ((), ())), preferred_element_type=f32)


def halves(x):
    high = x.astype(bf16)
    return high, (x - high.astype(f32)).astype(bf16)


def split_dot(a, b, ca, cb):
    rows = a[0].shape[1 - ca]
    both = dot(jnp.concatenate(a, axis=1 - ca), b[0], ca, cb)
    return both[:rows] + both[rows:] + dot(a[0], b[1], ca, cb)


def dot3(a, b, cb=1):
    return split_dot(halves(a), halves(b), 1, cb)


def features(x, y, z, is_source):
    row = lax.broadcasted_iota(jnp.int32, (FEATURES, PANELS), 0)
    dim = row % 3
    coord_row = row < 24
    x, y, z = (jnp.broadcast_to(value, (FEATURES, PANELS)) for value in (x, y, z))
    square = x * x + y * y + z * z
    value = jnp.where(dim == 0, x, jnp.where(dim == 1, y, z))
    pair = row // 3
    part = jnp.zeros_like(row)
    side = 0 if is_source else 1
    for index, parts in enumerate(PAIRS):
        if parts[side]:
            part = jnp.where(pair == index, parts[side], part)
    if is_source:
        value = jnp.where(coord_row, value, jnp.where(pair == 8, square, 1.0))
        part = jnp.where(pair == 8, dim, part)
    else:
        value = jnp.where(coord_row, -2.0 * value, jnp.where(pair == 8, 1.0, square + reg_square))
        part = jnp.where(pair == 9, dim, part)
    value = jnp.where(row < 30, value, 0.0)
    high = value.astype(bf16).astype(f32)
    rest = value - high
    middle = rest.astype(bf16).astype(f32)
    low = rest - middle
    return jnp.where(part == 0, high, jnp.where(part == 1, middle, low)).astype(bf16)


def place():
    b = lax.axis_index("branch")
    c = lax.axis_index("cluster")
    return b, c, c % 2, (c // 2) % NY, c // (2 * NY)


def remote(source_ref, target_ref, send_sem, recv_sem, index, peer):
    return pltpu.make_async_remote_copy(
        src_ref=source_ref,
        dst_ref=target_ref,
        send_sem=send_sem.at[index],
        recv_sem=recv_sem.at[index],
        device_id=peer,
        device_id_type=MESH,
    )


def greet(peers):
    barrier = pltpu.get_barrier_semaphore()
    for peer in peers:
        pl.semaphore_signal(barrier, inc=1, device_id=peer, device_id_type=MESH)
    return lambda: pl.semaphore_wait(barrier, len(peers))


def start_loads(pairs, sem):
    copies = [pltpu.make_async_copy(a, b, sem.at[i]) for i, (a, b) in enumerate(pairs)]
    for copy in copies:
        copy.start()
    return copies


def flipped(index):
    return index + 1 - 2 * (index % 2)


def pair_up(up_tr, level, left_child, right_child):
    return dot3(left_child, up_tr[level, 0]) + dot3(right_child, up_tr[level, 1])


def rows(nodes, picks):
    found = [nodes[SCEN * i : SCEN * i + SCEN] for i in picks]
    return found[0] if len(found) == 1 else jnp.concatenate(found, axis=0)


def exchange(
    charges_hbm,
    coords_hbm,
    areas_hbm,
    col_hbm,
    up_hbm,
    up_tr_hbm,
    down_hbm,
    row_hbm,
    down_tr_hbm,
    sibling_hbm,
    branch_hbm,
    source_out,
    weight_out,
    target_out,
    coef_out,
    pair_out,
    partner_out,
    way_out,
    high_out,
    low_out,
    charges,
    coords,
    areas,
    col,
    leaf_up,
    up_tr,
    leaf_down,
    rowb,
    down_tr,
    sibling,
    branch,
    node0,
    source,
    weight,
    target,
    coef,
    pair,
    partner0,
    way,
    down_high,
    down_low,
    local_sem,
    out_sem,
    send_sem,
    recv_sem,
):
    b, c, core, y, x = place()
    own = pl.ds(LEAVES, LEAVES)
    low_side, high_side = pl.ds(0, LEAVES), pl.ds(2 * LEAVES, LEAVES)
    left = (b, (c + CLUSTERS - 1) % CLUSTERS)
    right = (b, (c + 1) % CLUSTERS)
    partner = (b, flipped(c))
    wait_for_all = greet([left, right])

    loads = start_loads(
        (
            (coords_hbm, coords.at[:, own]),
            (areas_hbm, areas.at[own]),
            (charges_hbm, charges.at[own]),
            (col_hbm, col),
            (up_hbm, leaf_up),
            (up_tr_hbm, up_tr),
            (down_tr_hbm, down_tr),
            (sibling_hbm, sibling),
            (branch_hbm, branch),
            (down_hbm, leaf_down),
            (row_hbm, rowb),
        ),
        local_sem,
    )

    def send(source_ref, target_ref, index, peer):
        return remote(source_ref, target_ref, send_sem, recv_sem, index, peer)

    def sides(ref, index, lead):
        at = (lambda part: ref.at[:, part]) if lead else (lambda part: ref.at[part])
        return [send(at(own), at(high_side), index, left), send(at(own), at(low_side), index + 1, right)]

    coords_copies = sides(coords, 0, True)
    areas_copies = sides(areas, 2, False)
    charges_copies = sides(charges, 4, False)
    to_partner = send(node0, partner0, 6, partner)

    for index in range(3):
        loads[index].wait()
    wait_for_all()
    for copy in coords_copies + areas_copies + charges_copies:
        copy.start()

    loads[3].wait()

    @pl.loop(0, LEAVES // 8)
    def _(step):
        for inner in range(8):
            n = step * 8 + inner
            coef[n] = dot3(charges[LEAVES + n], col[n])

    loads[4].wait()

    def add_leaf(step, total):
        for inner in range(8):
            n = step * 8 + inner
            total = total + dot3(coef[n], leaf_up[n])
        return total

    node0[...] = lax.fori_loop(0, LEAVES // 8, add_leaf, jnp.zeros((SCEN, RANK), f32))
    to_partner.start()

    centres = []
    for i in range(3):
        mean = jnp.sum(coords[i, LEAVES : 2 * LEAVES], axis=0, keepdims=True)
        centres.append(jnp.sum(mean, axis=1, keepdims=True) * (1.0 / (LEAVES * PANELS)))

    def features_of(m, is_source):
        point = [coords[i, pl.ds(m, 1)] - centres[i] for i in range(3)]
        return features(*point, is_source)

    def weigh(m):
        high, low = halves(charges[m] * (areas[pl.ds(m, 1)] * inv_four_pi))
        weight[m, 0:SCEN] = high
        weight[m, SCEN : 2 * SCEN] = low

    @pl.loop(0, LEAVES // 2)
    def _(step):
        for inner in range(2):
            n = step * 2 + inner
            source[LEAVES + n] = features_of(LEAVES + n, True)
            target[n] = features_of(LEAVES + n, False)
            weigh(LEAVES + n)

    parts = []

    def store(ref, hbm):
        copy = pltpu.make_async_copy(ref, hbm, out_sem.at[len(parts)])
        copy.start()
        parts.append(copy)

    store(coef, coef_out)
    store(target, target_out)
    store(source.at[own], source_out.at[own])
    store(weight.at[own], weight_out.at[own])

    loads[5].wait()
    to_partner.wait()
    mine, other = node0[...], partner0[...]
    even = core == 0
    pair[...] = pair_up(up_tr, 0, jnp.where(even, mine, other), jnp.where(even, other, mine))
    store(pair, pair_out)
    store(partner0, partner_out)

    for index in range(6, 11):
        loads[index].wait()
    side = (core, y % 2, (y // 2) % 2, y // 4, x % 2, x // 2)
    way[0] = sibling[0, side[0]]
    path = down_tr[0, side[0]]
    for level in range(1, LEVELS):
        way[level] = dot3(path, sibling[level, side[level]], 0)
        path = dot3(path, down_tr[level, side[level]], 0)
    path_halves = halves(path)
    for i in range(NZ - 1):
        way[LEVELS + i] = split_dot(path_halves, halves(branch[i]), 1, 0)
    store(way, way_out)

    @pl.loop(0, LEAVES // 8)
    def _(step):
        for inner in range(8):
            n = step * 8 + inner
            product = split_dot(halves(leaf_down[n]), halves(rowb[n]), 0, 0)
            down_high[n], down_low[n] = halves(product)

    store(down_high, high_out)
    store(down_low, low_out)

    for copy in coords_copies:
        copy.wait()

    @pl.loop(0, LEAVES // 2)
    def _(step):
        for inner in range(2):
            n = step * 2 + inner
            source[n] = features_of(n, True)
            source[2 * LEAVES + n] = features_of(2 * LEAVES + n, True)

    store(source.at[low_side], source_out.at[low_side])
    store(source.at[high_side], source_out.at[high_side])
    for copy in areas_copies + charges_copies:
        copy.wait()

    @pl.loop(0, LEAVES // 4)
    def _(step):
        for inner in range(4):
            n = step * 4 + inner
            weigh(n)
            weigh(2 * LEAVES + n)

    store(weight.at[low_side], weight_out.at[low_side])
    store(weight.at[high_side], weight_out.at[high_side])
    for copy in parts:
        copy.wait()


def near_field(
    near_hbm,
    far_hbm,
    source_hbm,
    target_hbm,
    weight_hbm,
    coef_hbm,
    pair_hbm,
    partner_hbm,
    coupling_hbm,
    row_hbm,
    up_tr_hbm,
    way_hbm,
    high_hbm,
    low_hbm,
    out,
    near,
    far,
    source,
    target,
    weight,
    coef,
    partner0,
    coupling,
    rowb,
    up_tr,
    way,
    local,
    down_high,
    down_low,
    ynodes,
    nodes2,
    nodes3,
    xnodes,
    nodes5,
    roots,
    local_sem,
    send_sem,
    recv_sem,
):
    b, c, core, y, x = place()
    y_peers = [(b, (x * NY + (y + k) % NY) * 2 + core) for k in range(1, NY)]
    x_peers = [(b, (((x + k) % NX) * NY + y) * 2 + core) for k in range(1, NX)]
    z_peers = [((b + k) % NZ, c) for k in range(1, NZ)]
    left = (b, (c + CLUSTERS - 1) % CLUSTERS)
    right = (b, (c + 1) % CLUSTERS)
    own = pl.ds(LEAVES, LEAVES)
    wait_for_all = greet([left, right] + y_peers + x_peers + z_peers)
    loads = start_loads(
        (
            (near_hbm, near),
            (target_hbm, target),
            (source_hbm, source),
            (weight_hbm, weight),
            (pair_hbm, ynodes.at[y]),
            (up_tr_hbm, up_tr),
            (coef_hbm, coef.at[own]),
            (far_hbm, far),
            (coupling_hbm, coupling),
            (row_hbm, rowb),
            (partner_hbm, partner0),
            (way_hbm, way),
            (high_hbm, down_high),
            (low_hbm, down_low),
        ),
        local_sem,
    )

    def send(source_ref, target_ref, index, peer):
        return remote(source_ref, target_ref, send_sem, recv_sem, index, peer)

    to_y = [send(ynodes.at[y], ynodes.at[y], k, peer) for k, peer in enumerate(y_peers)]
    to_x = [send(xnodes.at[x], xnodes.at[x], 7 + k, peer) for k, peer in enumerate(x_peers)]
    to_z = [send(roots.at[b], roots.at[b], 10 + k, peer) for k, peer in enumerate(z_peers)]
    to_sides = [
        send(coef.at[own], coef.at[pl.ds(2 * LEAVES, LEAVES)], 17, left),
        send(coef.at[own], coef.at[pl.ds(0, LEAVES)], 18, right),
    ]
    for index in range(4):
        loads[index].wait()
    shift = LEAVES - (b * CLUSTERS + c) * LEAVES

    def window_index(leaf):
        return jnp.minimum(jnp.maximum(leaf + shift, 0), 3 * LEAVES - 1)

    @pl.loop(0, LEAVES // GROUP)
    def _(step):
        found = []
        for inner in range(GROUP):
            n = step * GROUP + inner
            tn = target[n]
            high_sum = jnp.zeros((2 * SCEN, PANELS), f32)
            low_sum = jnp.zeros((SCEN, PANELS), f32)
            for slot in range(NEAR):
                m = window_index(near[n, slot])
                kernel = lax.rsqrt(dot(source[m], tn, 0, 0))
                kernel_high, kernel_low = halves(kernel)
                wm = weight[m]
                high_sum = high_sum + dot(wm, kernel_high, 1, 0)
                low_sum = low_sum + dot(wm[:SCEN], kernel_low, 1, 0)
            found.append((n, high_sum[:SCEN] + high_sum[SCEN:] + low_sum))
        for n, value in found:
            out[n] = value

        @pl.when(step == BARRIER_AT)
        def _():
            loads[4].wait()
            loads[5].wait()
            loads[6].wait()
            wait_for_all()
            for copy in to_y + to_sides:
                copy.start()

        @pl.when(step == Y_AT)
        def _():
            for copy in to_y:
                copy.wait()
            level = jnp.concatenate([ynodes[i] for i in range(NY)], axis=0)
            level = pair_up(up_tr, 1, rows(level, (0, 2, 4, 6)), rows(level, (1, 3, 5, 7)))
            for i in range(4):
                nodes2[i] = rows(level, (i,))
            level = pair_up(up_tr, 2, rows(level, (0, 2)), rows(level, (1, 3)))
            for i in range(2):
                nodes3[i] = rows(level, (i,))
            xnodes[x] = pair_up(up_tr, 3, rows(level, (0,)), rows(level, (1,)))
            for copy in to_x:
                copy.start()

        @pl.when(step == X_AT)
        def _():
            for copy in to_x:
                copy.wait()
            level = jnp.concatenate([xnodes[i] for i in range(NX)], axis=0)
            level = pair_up(up_tr, 4, rows(level, (0, 2)), rows(level, (1, 3)))
            for i in range(2):
                nodes5[i] = rows(level, (i,))
            roots[b] = pair_up(up_tr, 5, rows(level, (0,)), rows(level, (1,)))
            for copy in to_z:
                copy.start()

    for index in range(7, 14):
        loads[index].wait()
    for copy in to_sides:
        copy.wait()

    for n in range(LEAVES):
        total = jnp.zeros((SCEN, RANK), f32)
        for slot in range(FAR):
            total = total + dot3(coef[window_index(far[slot, n])], coupling[n, slot])
        local[n] = total
    for n in range(LEAVES):
        out[n] = out[n] + split_dot(halves(local[n]), halves(rowb[n]), 1, 0)

    siblings = (
        partner0[...],
        ynodes[flipped(y)],
        nodes2[flipped(y // 2)],
        nodes3[flipped(y // 4)],
        xnodes[flipped(x)],
        nodes5[flipped(x // 2)],
    )
    down = jnp.zeros((SCEN, RANK), f32)
    for level in range(LEVELS):
        down = down + dot3(siblings[level], way[level])
    for copy in to_z:
        copy.wait()
    for i in range(NZ - 1):
        down = down + dot3(roots[(b + 1 + i) % NZ], way[LEVELS + i])
    halved = halves(down)

    @pl.loop(0, LEAVES // 8)
    def _(step):
        for inner in range(8):
            n = step * 8 + inner
            out[n] = out[n] + split_dot(halved, (down_high[n], down_low[n]), 1, 0)


def on_device(charges, coords, areas, col, row, up, down, coupling, up_tr, down_tr, sib, branch, near, far):
    window = 3 * LEAVES
    hbm = pl.BlockSpec(memory_space=pltpu.HBM)
    node = (SCEN, RANK)
    square = (RANK, RANK)
    leaf_shape = (LEAVES, SCEN, PANELS)
    down_shape = (LEAVES, RANK, PANELS)
    made = (
        ((window, FEATURES, PANELS), bf16),
        ((window, 2 * SCEN, PANELS), bf16),
        ((LEAVES, FEATURES, PANELS), bf16),
        ((LEAVES,) + node, f32),
        (node, f32),
        (node, f32),
        ((LEVELS + NZ - 1,) + square, f32),
        (down_shape, bf16),
        (down_shape, bf16),
    )

    def vmem(*shape):
        return pltpu.VMEM(shape, f32)

    def params(collective_id, limit):
        return pltpu.CompilerParams(
            collective_id=collective_id, has_side_effects=True, vmem_limit_bytes=limit
        )

    scratch = [pltpu.VMEM(shape, kind) for shape, kind in made]
    transfer = vmem(LEVELS, 2, *square)
    source, weight, target, coef, pair, partner, way, high, low = pl.pallas_call(
        exchange,
        out_shape=[jax.ShapeDtypeStruct(shape, kind) for shape, kind in made],
        in_specs=[hbm] * 11,
        out_specs=[hbm] * 9,
        scratch_shapes=[
            vmem(window, SCEN, PANELS),
            vmem(3, window, PANELS),
            vmem(window, PANELS),
            vmem(LEAVES, RANK, PANELS),
            vmem(LEAVES, *square),
            transfer,
            vmem(LEAVES, *square),
            vmem(LEAVES, RANK, PANELS),
            transfer,
            transfer,
            vmem(NZ - 1, *square),
            vmem(*node),
        ]
        + scratch
        + [
            pltpu.SemaphoreType.DMA((11,)),
            pltpu.SemaphoreType.DMA((13,)),
            pltpu.SemaphoreType.DMA((7,)),
            pltpu.SemaphoreType.DMA((7,)),
        ],
        compiler_params=params(0, FULL_VMEM),
        name="exchange",
    )(
        charges,
        jnp.transpose(coords, (1, 0, 2)),
        areas,
        col,
        up,
        up_tr[0],
        down,
        row,
        down_tr[0],
        sib[0],
        branch[0],
    )
    return pl.pallas_call(
        near_field,
        out_shape=jax.ShapeDtypeStruct(leaf_shape, f32),
        in_specs=[hbm] * 14,
        out_specs=pl.BlockSpec(memory_space=pltpu.VMEM),
        scratch_shapes=[
            pltpu.SMEM((LEAVES, NEAR), jnp.int32),
            pltpu.SMEM((FAR, LEAVES), jnp.int32),
            scratch[0],
            scratch[2],
            scratch[1],
            vmem(window, *node),
            scratch[5],
            vmem(LEAVES, FAR, *square),
            vmem(LEAVES, RANK, PANELS),
            transfer,
            scratch[6],
            vmem(LEAVES, *node),
            pltpu.VMEM(down_shape, bf16),
            pltpu.VMEM(down_shape, bf16),
            vmem(NY, *node),
            vmem(4, *node),
            vmem(2, *node),
            vmem(NX, *node),
            vmem(2, *node),
            vmem(NZ, *node),
            pltpu.SemaphoreType.DMA((14,)),
            pltpu.SemaphoreType.DMA((19,)),
            pltpu.SemaphoreType.DMA((19,)),
        ],
        compiler_params=params(1, FULL_VMEM),
        name="near_field",
    )(
        near,
        far.T,
        source,
        target,
        weight,
        coef,
        pair,
        partner,
        coupling,
        row,
        up_tr[0],
        way,
        high,
        low,
    )


def solution(mesh):
    leaf = ("branch", "cluster")

    def spec(axis, rank):
        return P(axis, *([None] * (rank - 1)))

    in_specs = (
        spec(leaf, 3),
        spec(leaf, 3),
        spec(leaf, 2),
        spec(leaf, 3),
        spec(leaf, 3),
        spec(leaf, 3),
        spec(leaf, 3),
        spec(leaf, 4),
        spec("branch", 5),
        spec("branch", 5),
        spec("branch", 5),
        spec("branch", 4),
        spec(leaf, 2),
        spec(leaf, 2),
    )
    return jax.shard_map(
        on_device, mesh=mesh, in_specs=in_specs, out_specs=spec(leaf, 3), check_vma=False
    )
```

```python
import functools
import math

import jax
import jax.numpy as jnp
from jax import lax
from jax.experimental import pallas as pl
from jax.experimental.pallas import tpu as pltpu
from jax.sharding import PartitionSpec as P

f32, bf16 = jnp.float32, jnp.bfloat16
MESH = pl.DeviceIdType.MESH
reg_square = 0.01
inv_four_pi = 0.25 / math.pi

LEAVES, SCEN, PANELS, RANK = 16, 16, 256, 64
NEAR, FAR, LEVELS = 16, 4, 6
NX, NY, NZ, CLUSTERS = 4, 8, 8, 64
FEATURES = 32
KERNEL_VMEM = 67043328 - (6 << 20)
GROUP = 2
BARRIER_AT, Y_AT, X_AT = 2, 3, 4
PAIRS = ((0, 0), (0, 1), (1, 0), (0, 2), (2, 0), (1, 1), (1, 2), (2, 1))


def dot(a, b, ca, cb):
    return lax.dot_general(a, b, (((ca,), (cb,)), ((), ())), preferred_element_type=f32)


def halves(x):
    high = x.astype(bf16)
    return high, (x - high.astype(f32)).astype(bf16)


def split_dot(a, b, ca, cb):
    rows = a[0].shape[1 - ca]
    both = dot(jnp.concatenate(a, axis=1 - ca), b[0], ca, cb)
    return both[:rows] + both[rows:] + dot(a[0], b[1], ca, cb)


def dot3(a, b, cb=1):
    return split_dot(halves(a), halves(b), 1, cb)


def features(x, y, z, is_source):
    row = lax.broadcasted_iota(jnp.int32, (FEATURES, PANELS), 0)
    dim = row % 3
    coord_row = row < 24
    x, y, z = (jnp.broadcast_to(value, (FEATURES, PANELS)) for value in (x, y, z))
    square = x * x + y * y + z * z
    value = jnp.where(dim == 0, x, jnp.where(dim == 1, y, z))
    pair = row // 3
    part = jnp.zeros_like(row)
    side = 0 if is_source else 1
    for index, parts in enumerate(PAIRS):
        if parts[side]:
            part = jnp.where(pair == index, parts[side], part)
    if is_source:
        value = jnp.where(coord_row, value, jnp.where(pair == 8, square, 1.0))
        part = jnp.where(pair == 8, dim, part)
    else:
        value = jnp.where(coord_row, -2.0 * value, jnp.where(pair == 8, 1.0, square + reg_square))
        part = jnp.where(pair == 9, dim, part)
    value = jnp.where(row < 30, value, 0.0)
    high = value.astype(bf16).astype(f32)
    rest = value - high
    middle = rest.astype(bf16).astype(f32)
    low = rest - middle
    return jnp.where(part == 0, high, jnp.where(part == 1, middle, low)).astype(bf16)


def place():
    b = lax.axis_index("branch")
    c = lax.axis_index("cluster")
    return b, c, c % 2, (c // 2) % NY, c // (2 * NY)


def remote(source_ref, target_ref, send_sem, recv_sem, index, peer):
    return pltpu.make_async_remote_copy(
        src_ref=source_ref,
        dst_ref=target_ref,
        send_sem=send_sem.at[index],
        recv_sem=recv_sem.at[index],
        device_id=peer,
        device_id_type=MESH,
    )


def greet(peers):
    barrier = pltpu.get_barrier_semaphore()
    for peer in peers:
        pl.semaphore_signal(barrier, inc=1, device_id=peer, device_id_type=MESH)
    return lambda: pl.semaphore_wait(barrier, len(peers))


def start_loads(pairs, sem):
    copies = [pltpu.make_async_copy(a, b, sem.at[i]) for i, (a, b) in enumerate(pairs)]
    for copy in copies:
        copy.start()
    return copies


def flipped(index):
    return index + 1 - 2 * (index % 2)


def pair_up(up_tr, level, left_child, right_child):
    return dot3(left_child, up_tr[level, 0]) + dot3(right_child, up_tr[level, 1])


def rows(nodes, picks):
    found = [nodes[SCEN * i : SCEN * i + SCEN] for i in picks]
    return found[0] if len(found) == 1 else jnp.concatenate(found, axis=0)


def exchange(
    charges_hbm,
    coords_hbm,
    areas_hbm,
    col_hbm,
    up_hbm,
    up_tr_hbm,
    down_hbm,
    row_hbm,
    down_tr_hbm,
    sibling_hbm,
    branch_hbm,
    source,
    weight,
    target,
    coef,
    pair,
    partner_out,
    way,
    down_high,
    down_low,
    charges,
    coords,
    areas,
    col,
    leaf_up,
    up_tr,
    leaf_down,
    rowb,
    down_tr,
    sibling,
    branch,
    node0,
    partner0,
    local_sem,
    send_sem,
    recv_sem,
):
    b, c, core, y, x = place()
    own = pl.ds(LEAVES, LEAVES)
    low_side, high_side = pl.ds(0, LEAVES), pl.ds(2 * LEAVES, LEAVES)
    left = (b, (c + CLUSTERS - 1) % CLUSTERS)
    right = (b, (c + 1) % CLUSTERS)
    partner = (b, flipped(c))
    wait_for_all = greet([left, right])

    loads = start_loads(
        (
            (coords_hbm, coords.at[:, own]),
            (areas_hbm, areas.at[own]),
            (charges_hbm, charges.at[own]),
            (col_hbm, col),
            (up_hbm, leaf_up),
            (up_tr_hbm, up_tr),
            (down_tr_hbm, down_tr),
            (sibling_hbm, sibling),
            (branch_hbm, branch),
            (down_hbm, leaf_down),
            (row_hbm, rowb),
        ),
        local_sem,
    )

    def send(source_ref, target_ref, index, peer):
        return remote(source_ref, target_ref, send_sem, recv_sem, index, peer)

    def sides(ref, index, lead):
        at = (lambda part: ref.at[:, part]) if lead else (lambda part: ref.at[part])
        return [send(at(own), at(high_side), index, left), send(at(own), at(low_side), index + 1, right)]

    coords_copies = sides(coords, 0, True)
    areas_copies = sides(areas, 2, False)
    charges_copies = sides(charges, 4, False)
    to_partner = send(node0, partner0, 6, partner)

    for index in range(3):
        loads[index].wait()
    wait_for_all()
    for copy in coords_copies + areas_copies + charges_copies:
        copy.start()

    loads[3].wait()

    @pl.loop(0, LEAVES // 8)
    def _(step):
        for inner in range(8):
            n = step * 8 + inner
            coef[n] = dot3(charges[LEAVES + n], col[n])

    loads[4].wait()

    def add_leaf(step, total):
        for inner in range(8):
            n = step * 8 + inner
            total = total + dot3(coef[n], leaf_up[n])
        return total

    node0[...] = lax.fori_loop(0, LEAVES // 8, add_leaf, jnp.zeros((SCEN, RANK), f32))
    to_partner.start()

    centres = []
    for i in range(3):
        mean = jnp.sum(coords[i, LEAVES : 2 * LEAVES], axis=0, keepdims=True)
        centres.append(jnp.sum(mean, axis=1, keepdims=True) * (1.0 / (LEAVES * PANELS)))

    def features_of(m, is_source):
        point = [coords[i, pl.ds(m, 1)] - centres[i] for i in range(3)]
        return features(*point, is_source)

    def weigh(m):
        high, low = halves(charges[m] * (areas[pl.ds(m, 1)] * inv_four_pi))
        weight[m, 0:SCEN] = high
        weight[m, SCEN : 2 * SCEN] = low

    @pl.loop(0, LEAVES // 2)
    def _(step):
        for inner in range(2):
            n = step * 2 + inner
            source[LEAVES + n] = features_of(LEAVES + n, True)
            target[n] = features_of(LEAVES + n, False)
            weigh(LEAVES + n)

    loads[5].wait()
    to_partner.wait()
    mine, other = node0[...], partner0[...]
    even = core == 0
    pair[...] = pair_up(up_tr, 0, jnp.where(even, mine, other), jnp.where(even, other, mine))
    partner_out[...] = other

    for index in range(6, 11):
        loads[index].wait()
    side = (core, y % 2, (y // 2) % 2, y // 4, x % 2, x // 2)
    way[0] = sibling[0, side[0]]
    path = down_tr[0, side[0]]
    for level in range(1, LEVELS):
        way[level] = dot3(path, sibling[level, side[level]], 0)
        path = dot3(path, down_tr[level, side[level]], 0)
    path_halves = halves(path)
    for i in range(NZ - 1):
        way[LEVELS + i] = split_dot(path_halves, halves(branch[i]), 1, 0)

    @pl.loop(0, LEAVES // 8)
    def _(step):
        for inner in range(8):
            n = step * 8 + inner
            product = split_dot(halves(leaf_down[n]), halves(rowb[n]), 0, 0)
            down_high[n], down_low[n] = halves(product)


    for copy in coords_copies:
        copy.wait()

    @pl.loop(0, LEAVES // 2)
    def _(step):
        for inner in range(2):
            n = step * 2 + inner
            source[n] = features_of(n, True)
            source[2 * LEAVES + n] = features_of(2 * LEAVES + n, True)

    for copy in areas_copies + charges_copies:
        copy.wait()

    @pl.loop(0, LEAVES // 4)
    def _(step):
        for inner in range(4):
            n = step * 4 + inner
            weigh(n)
            weigh(2 * LEAVES + n)


def near_field(
    near_hbm,
    far_hbm,
    source,
    target,
    weight,
    own_coef,
    pair,
    partner0,
    coupling_hbm,
    row_hbm,
    up_tr_hbm,
    way,
    down_high,
    down_low,
    out,
    near,
    far,
    coef,
    coupling,
    rowb,
    up_tr,
    local,
    ynodes,
    nodes2,
    nodes3,
    xnodes,
    nodes5,
    roots,
    local_sem,
    send_sem,
    recv_sem,
):
    b, c, core, y, x = place()
    y_peers = [(b, (x * NY + (y + k) % NY) * 2 + core) for k in range(1, NY)]
    x_peers = [(b, (((x + k) % NX) * NY + y) * 2 + core) for k in range(1, NX)]
    z_peers = [((b + k) % NZ, c) for k in range(1, NZ)]
    left = (b, (c + CLUSTERS - 1) % CLUSTERS)
    right = (b, (c + 1) % CLUSTERS)
    own = pl.ds(LEAVES, LEAVES)
    wait_for_all = greet([left, right] + y_peers + x_peers + z_peers)
    loads = start_loads(
        (
            (near_hbm, near),
            (up_tr_hbm, up_tr),
            (far_hbm, far),
            (coupling_hbm, coupling),
            (row_hbm, rowb),
        ),
        local_sem,
    )

    def send(source_ref, target_ref, index, peer):
        return remote(source_ref, target_ref, send_sem, recv_sem, index, peer)

    to_y = [send(ynodes.at[y], ynodes.at[y], k, peer) for k, peer in enumerate(y_peers)]
    to_x = [send(xnodes.at[x], xnodes.at[x], 7 + k, peer) for k, peer in enumerate(x_peers)]
    to_z = [send(roots.at[b], roots.at[b], 10 + k, peer) for k, peer in enumerate(z_peers)]
    to_sides = [
        send(coef.at[own], coef.at[pl.ds(2 * LEAVES, LEAVES)], 17, left),
        send(coef.at[own], coef.at[pl.ds(0, LEAVES)], 18, right),
    ]
    ynodes[y] = pair[...]
    coef[own] = own_coef[...]
    loads[0].wait()
    shift = LEAVES - (b * CLUSTERS + c) * LEAVES

    def window_index(leaf):
        return jnp.minimum(jnp.maximum(leaf + shift, 0), 3 * LEAVES - 1)

    @pl.loop(0, LEAVES // GROUP)
    def _(step):
        found = []
        for inner in range(GROUP):
            n = step * GROUP + inner
            tn = target[n]
            high_sum = jnp.zeros((2 * SCEN, PANELS), f32)
            low_sum = jnp.zeros((SCEN, PANELS), f32)
            for slot in range(NEAR):
                m = window_index(near[n, slot])
                kernel = lax.rsqrt(dot(source[m], tn, 0, 0))
                kernel_high, kernel_low = halves(kernel)
                wm = weight[m]
                high_sum = high_sum + dot(wm, kernel_high, 1, 0)
                low_sum = low_sum + dot(wm[:SCEN], kernel_low, 1, 0)
            found.append((n, high_sum[:SCEN] + high_sum[SCEN:] + low_sum))
        for n, value in found:
            out[n] = value

        @pl.when(step == BARRIER_AT)
        def _():
            loads[1].wait()
            wait_for_all()
            for copy in to_y + to_sides:
                copy.start()

        @pl.when(step == Y_AT)
        def _():
            for copy in to_y:
                copy.wait()
            level = jnp.concatenate([ynodes[i] for i in range(NY)], axis=0)
            level = pair_up(up_tr, 1, rows(level, (0, 2, 4, 6)), rows(level, (1, 3, 5, 7)))
            for i in range(4):
                nodes2[i] = rows(level, (i,))
            level = pair_up(up_tr, 2, rows(level, (0, 2)), rows(level, (1, 3)))
            for i in range(2):
                nodes3[i] = rows(level, (i,))
            xnodes[x] = pair_up(up_tr, 3, rows(level, (0,)), rows(level, (1,)))
            for copy in to_x:
                copy.start()

        @pl.when(step == X_AT)
        def _():
            for copy in to_x:
                copy.wait()
            level = jnp.concatenate([xnodes[i] for i in range(NX)], axis=0)
            level = pair_up(up_tr, 4, rows(level, (0, 2)), rows(level, (1, 3)))
            for i in range(2):
                nodes5[i] = rows(level, (i,))
            roots[b] = pair_up(up_tr, 5, rows(level, (0,)), rows(level, (1,)))
            for copy in to_z:
                copy.start()

    for index in range(2, 5):
        loads[index].wait()
    for copy in to_sides:
        copy.wait()

    for n in range(LEAVES):
        total = jnp.zeros((SCEN, RANK), f32)
        for slot in range(FAR):
            total = total + dot3(coef[window_index(far[slot, n])], coupling[n, slot])
        local[n] = total
    for n in range(LEAVES):
        out[n] = out[n] + split_dot(halves(local[n]), halves(rowb[n]), 1, 0)

    siblings = (
        partner0[...],
        ynodes[flipped(y)],
        nodes2[flipped(y // 2)],
        nodes3[flipped(y // 4)],
        xnodes[flipped(x)],
        nodes5[flipped(x // 2)],
    )
    down = jnp.zeros((SCEN, RANK), f32)
    for level in range(LEVELS):
        down = down + dot3(siblings[level], way[level])
    for copy in to_z:
        copy.wait()
    for i in range(NZ - 1):
        down = down + dot3(roots[(b + 1 + i) % NZ], way[LEVELS + i])
    halved = halves(down)

    @pl.loop(0, LEAVES // 8)
    def _(step):
        for inner in range(8):
            n = step * 8 + inner
            out[n] = out[n] + split_dot(halved, (down_high[n], down_low[n]), 1, 0)


def on_device(charges, coords, areas, col, row, up, down, coupling, up_tr, down_tr, sib, branch, near, far):
    window = 3 * LEAVES
    hbm = pl.BlockSpec(memory_space=pltpu.HBM)
    node = (SCEN, RANK)
    square = (RANK, RANK)
    leaf_shape = (LEAVES, SCEN, PANELS)
    down_shape = (LEAVES, RANK, PANELS)
    made = (
        ((window, FEATURES, PANELS), bf16),
        ((window, 2 * SCEN, PANELS), bf16),
        ((LEAVES, FEATURES, PANELS), bf16),
        ((LEAVES,) + node, f32),
        (node, f32),
        (node, f32),
        ((LEVELS + NZ - 1,) + square, f32),
        (down_shape, bf16),
        (down_shape, bf16),
    )

    def vmem(*shape):
        return pltpu.VMEM(shape, f32)

    def params(collective_id, limit):
        return pltpu.CompilerParams(
            collective_id=collective_id, has_side_effects=True, vmem_limit_bytes=limit
        )

    passed = [pltpu.VMEM(shape, kind) for shape, kind in made]
    on_chip = pl.BlockSpec(memory_space=pltpu.VMEM)
    transfer = vmem(LEVELS, 2, *square)
    source, weight, target, coef, pair, partner, way, high, low = pl.pallas_call(
        exchange,
        out_shape=passed,
        in_specs=[hbm] * 11,
        out_specs=[on_chip] * 9,
        scratch_shapes=[
            vmem(window, SCEN, PANELS),
            vmem(3, window, PANELS),
            vmem(window, PANELS),
            vmem(LEAVES, RANK, PANELS),
            vmem(LEAVES, *square),
            transfer,
            vmem(LEAVES, *square),
            vmem(LEAVES, RANK, PANELS),
            transfer,
            transfer,
            vmem(NZ - 1, *square),
            vmem(*node),
            vmem(*node),
            pltpu.SemaphoreType.DMA((11,)),
            pltpu.SemaphoreType.DMA((7,)),
            pltpu.SemaphoreType.DMA((7,)),
        ],
        compiler_params=params(0, KERNEL_VMEM),
        name="exchange",
    )(
        charges,
        jnp.transpose(coords, (1, 0, 2)),
        areas,
        col,
        up,
        up_tr[0],
        down,
        row,
        down_tr[0],
        sib[0],
        branch[0],
    )
    source, weight, target, coef, pair, partner, way, high, low = (
        pltpu.with_memory_space_constraint(array, pltpu.VMEM)
        for array in (source, weight, target, coef, pair, partner, way, high, low)
    )
    return pl.pallas_call(
        near_field,
        out_shape=pltpu.VMEM(leaf_shape, f32),
        in_specs=[hbm] * 2 + [on_chip] * 6 + [hbm] * 3 + [on_chip] * 3,
        out_specs=on_chip,
        scratch_shapes=[
            pltpu.SMEM((LEAVES, NEAR), jnp.int32),
            pltpu.SMEM((FAR, LEAVES), jnp.int32),
            vmem(window, *node),
            vmem(LEAVES, FAR, *square),
            vmem(LEAVES, RANK, PANELS),
            transfer,
            vmem(LEAVES, *node),
            vmem(NY, *node),
            vmem(4, *node),
            vmem(2, *node),
            vmem(NX, *node),
            vmem(2, *node),
            vmem(NZ, *node),
            pltpu.SemaphoreType.DMA((5,)),
            pltpu.SemaphoreType.DMA((19,)),
            pltpu.SemaphoreType.DMA((19,)),
        ],
        compiler_params=params(1, KERNEL_VMEM),
        name="near_field",
    )(
        near,
        far.T,
        source,
        target,
        weight,
        coef,
        pair,
        partner,
        coupling,
        row,
        up_tr[0],
        way,
        high,
        low,
    )


def solution(mesh):
    leaf = ("branch", "cluster")

    def spec(axis, rank):
        return P(axis, *([None] * (rank - 1)))

    in_specs = (
        spec(leaf, 3),
        spec(leaf, 3),
        spec(leaf, 2),
        spec(leaf, 3),
        spec(leaf, 3),
        spec(leaf, 3),
        spec(leaf, 3),
        spec(leaf, 4),
        spec("branch", 5),
        spec("branch", 5),
        spec("branch", 5),
        spec("branch", 4),
        spec(leaf, 2),
        spec(leaf, 2),
    )
    return jax.shard_map(
        on_device, mesh=mesh, in_specs=in_specs, out_specs=spec(leaf, 3), check_vma=False
    )
```

```python
import functools
import math

import jax
import jax.numpy as jnp
from jax import lax
from jax.experimental import pallas as pl
from jax.experimental.pallas import tpu as pltpu
from jax.sharding import PartitionSpec as P

f32, bf16 = jnp.float32, jnp.bfloat16
MESH = pl.DeviceIdType.MESH
reg_square = 0.01
inv_four_pi = 0.25 / math.pi

LEAVES, SCEN, PANELS, RANK = 16, 16, 256, 64
NEAR, FAR, LEVELS = 16, 4, 6
NX, NY, NZ, CLUSTERS = 4, 8, 8, 64
FEATURES = 32
KERNEL_VMEM = 67043328 - (6 << 20)
GROUP = 2
BARRIER_AT, Y_AT, X_AT = 2, 4, 5
PAIRS = ((0, 0), (0, 1), (1, 0), (0, 2), (2, 0), (1, 1), (1, 2), (2, 1))


def dot(a, b, ca, cb):
    return lax.dot_general(a, b, (((ca,), (cb,)), ((), ())), preferred_element_type=f32)


def halves(x):
    high = x.astype(bf16)
    return high, (x - high.astype(f32)).astype(bf16)


def split_dot(a, b, ca, cb):
    rows = a[0].shape[1 - ca]
    both = dot(jnp.concatenate(a, axis=1 - ca), b[0], ca, cb)
    return both[:rows] + both[rows:] + dot(a[0], b[1], ca, cb)


def dot3(a, b, cb=1):
    return split_dot(halves(a), halves(b), 1, cb)


def features(x, y, z, is_source):
    row = lax.broadcasted_iota(jnp.int32, (FEATURES, PANELS), 0)
    dim = row % 3
    coord_row = row < 24
    x, y, z = (jnp.broadcast_to(value, (FEATURES, PANELS)) for value in (x, y, z))
    square = x * x + y * y + z * z
    value = jnp.where(dim == 0, x, jnp.where(dim == 1, y, z))
    pair = row // 3
    part = jnp.zeros_like(row)
    side = 0 if is_source else 1
    for index, parts in enumerate(PAIRS):
        if parts[side]:
            part = jnp.where(pair == index, parts[side], part)
    if is_source:
        value = jnp.where(coord_row, value, jnp.where(pair == 8, square, 1.0))
        part = jnp.where(pair == 8, dim, part)
    else:
        value = jnp.where(coord_row, -2.0 * value, jnp.where(pair == 8, 1.0, square + reg_square))
        part = jnp.where(pair == 9, dim, part)
    value = jnp.where(row < 30, value, 0.0)
    high = value.astype(bf16).astype(f32)
    rest = value - high
    middle = rest.astype(bf16).astype(f32)
    low = rest - middle
    return jnp.where(part == 0, high, jnp.where(part == 1, middle, low)).astype(bf16)


def place():
    b = lax.axis_index("branch")
    c = lax.axis_index("cluster")
    return b, c, c % 2, (c // 2) % NY, c // (2 * NY)


def remote(source_ref, target_ref, send_sem, recv_sem, index, peer):
    return pltpu.make_async_remote_copy(
        src_ref=source_ref,
        dst_ref=target_ref,
        send_sem=send_sem.at[index],
        recv_sem=recv_sem.at[index],
        device_id=peer,
        device_id_type=MESH,
    )


def greet(peers):
    barrier = pltpu.get_barrier_semaphore()
    for peer in peers:
        pl.semaphore_signal(barrier, inc=1, device_id=peer, device_id_type=MESH)
    return lambda: pl.semaphore_wait(barrier, len(peers))


def start_loads(pairs, sem):
    copies = [pltpu.make_async_copy(a, b, sem.at[i]) for i, (a, b) in enumerate(pairs)]
    for copy in copies:
        copy.start()
    return copies


def flipped(index):
    return index + 1 - 2 * (index % 2)


def pair_up(up_tr, level, left_child, right_child):
    return dot3(left_child, up_tr[level, 0]) + dot3(right_child, up_tr[level, 1])


def rows(nodes, picks):
    found = [nodes[SCEN * i : SCEN * i + SCEN] for i in picks]
    return found[0] if len(found) == 1 else jnp.concatenate(found, axis=0)


def exchange(
    charges_hbm,
    coords_hbm,
    areas_hbm,
    col_hbm,
    up_hbm,
    up_tr_hbm,
    down_hbm,
    row_hbm,
    down_tr_hbm,
    sibling_hbm,
    branch_hbm,
    source,
    weight,
    target,
    coef,
    pair,
    partner_out,
    way,
    down_high,
    down_low,
    charges,
    coords,
    areas,
    col,
    leaf_up,
    up_tr,
    leaf_down,
    rowb,
    down_tr,
    sibling,
    branch,
    node0,
    partner0,
    local_sem,
    send_sem,
    recv_sem,
):
    b, c, core, y, x = place()
    own = pl.ds(LEAVES, LEAVES)
    low_side, high_side = pl.ds(0, LEAVES), pl.ds(2 * LEAVES, LEAVES)
    left = (b, (c + CLUSTERS - 1) % CLUSTERS)
    right = (b, (c + 1) % CLUSTERS)
    partner = (b, flipped(c))
    wait_for_all = greet([left, right])

    loads = start_loads(
        (
            (coords_hbm, coords.at[:, own]),
            (areas_hbm, areas.at[own]),
            (charges_hbm, charges.at[own]),
            (col_hbm, col),
            (up_hbm, leaf_up),
            (up_tr_hbm, up_tr),
            (down_tr_hbm, down_tr),
            (sibling_hbm, sibling),
            (branch_hbm, branch),
            (down_hbm, leaf_down),
            (row_hbm, rowb),
        ),
        local_sem,
    )

    def send(source_ref, target_ref, index, peer):
        return remote(source_ref, target_ref, send_sem, recv_sem, index, peer)

    def sides(ref, index, lead):
        at = (lambda part: ref.at[:, part]) if lead else (lambda part: ref.at[part])
        return [send(at(own), at(high_side), index, left), send(at(own), at(low_side), index + 1, right)]

    coords_copies = sides(coords, 0, True)
    areas_copies = sides(areas, 2, False)
    charges_copies = sides(charges, 4, False)
    to_partner = send(node0, partner0, 6, partner)

    for index in range(3):
        loads[index].wait()
    wait_for_all()
    for copy in coords_copies + areas_copies + charges_copies:
        copy.start()

    loads[3].wait()

    @pl.loop(0, LEAVES // 8)
    def _(step):
        for inner in range(8):
            n = step * 8 + inner
            coef[n] = dot3(charges[LEAVES + n], col[n])

    loads[4].wait()

    def add_leaf(step, total):
        for inner in range(8):
            n = step * 8 + inner
            total = total + dot3(coef[n], leaf_up[n])
        return total

    node0[...] = lax.fori_loop(0, LEAVES // 8, add_leaf, jnp.zeros((SCEN, RANK), f32))
    to_partner.start()

    centres = []
    for i in range(3):
        mean = jnp.sum(coords[i, LEAVES : 2 * LEAVES], axis=0, keepdims=True)
        centres.append(jnp.sum(mean, axis=1, keepdims=True) * (1.0 / (LEAVES * PANELS)))

    def features_of(m, is_source):
        point = [coords[i, pl.ds(m, 1)] - centres[i] for i in range(3)]
        return features(*point, is_source)

    def weigh(m):
        high, low = halves(charges[m] * (areas[pl.ds(m, 1)] * inv_four_pi))
        weight[m, 0:SCEN] = high
        weight[m, SCEN : 2 * SCEN] = low

    @pl.loop(0, LEAVES // 2)
    def _(step):
        for inner in range(2):
            n = step * 2 + inner
            source[LEAVES + n] = features_of(LEAVES + n, True)
            target[n] = features_of(LEAVES + n, False)
            weigh(LEAVES + n)

    loads[5].wait()
    to_partner.wait()
    mine, other = node0[...], partner0[...]
    even = core == 0
    pair[...] = pair_up(up_tr, 0, jnp.where(even, mine, other), jnp.where(even, other, mine))
    partner_out[...] = other

    for index in range(6, 11):
        loads[index].wait()
    side = (core, y % 2, (y // 2) % 2, y // 4, x % 2, x // 2)
    way[0] = sibling[0, side[0]]
    path = down_tr[0, side[0]]
    for level in range(1, LEVELS):
        way[level] = dot3(path, sibling[level, side[level]], 0)
        path = dot3(path, down_tr[level, side[level]], 0)
    path_halves = halves(path)
    for i in range(NZ - 1):
        way[LEVELS + i] = split_dot(path_halves, halves(branch[i]), 1, 0)

    @pl.loop(0, LEAVES // 8)
    def _(step):
        for inner in range(8):
            n = step * 8 + inner
            product = split_dot(halves(leaf_down[n]), halves(rowb[n]), 0, 0)
            down_high[n], down_low[n] = halves(product)


    for copy in coords_copies:
        copy.wait()

    @pl.loop(0, LEAVES // 2)
    def _(step):
        for inner in range(2):
            n = step * 2 + inner
            source[n] = features_of(n, True)
            source[2 * LEAVES + n] = features_of(2 * LEAVES + n, True)

    for copy in areas_copies + charges_copies:
        copy.wait()

    @pl.loop(0, LEAVES // 4)
    def _(step):
        for inner in range(4):
            n = step * 4 + inner
            weigh(n)
            weigh(2 * LEAVES + n)


def near_field(
    near_hbm,
    far_hbm,
    source,
    target,
    weight,
    own_coef,
    pair,
    partner0,
    coupling_hbm,
    row_hbm,
    up_tr_hbm,
    way,
    down_high,
    down_low,
    out,
    near,
    far,
    coef,
    coupling,
    rowb,
    up_tr,
    local,
    ynodes,
    nodes2,
    nodes3,
    xnodes,
    nodes5,
    roots,
    local_sem,
    send_sem,
    recv_sem,
):
    b, c, core, y, x = place()
    y_peers = [(b, (x * NY + (y + k) % NY) * 2 + core) for k in range(1, NY)]
    x_peers = [(b, (((x + k) % NX) * NY + y) * 2 + core) for k in range(1, NX)]
    z_peers = [((b + k) % NZ, c) for k in range(1, NZ)]
    left = (b, (c + CLUSTERS - 1) % CLUSTERS)
    right = (b, (c + 1) % CLUSTERS)
    own = pl.ds(LEAVES, LEAVES)
    wait_for_all = greet([left, right] + y_peers + x_peers + z_peers)
    loads = start_loads(
        (
            (near_hbm, near),
            (up_tr_hbm, up_tr),
            (far_hbm, far),
            (coupling_hbm, coupling),
            (row_hbm, rowb),
        ),
        local_sem,
    )

    def send(source_ref, target_ref, index, peer):
        return remote(source_ref, target_ref, send_sem, recv_sem, index, peer)

    to_y = [send(ynodes.at[y], ynodes.at[y], k, peer) for k, peer in enumerate(y_peers)]
    to_x = [send(xnodes.at[x], xnodes.at[x], 7 + k, peer) for k, peer in enumerate(x_peers)]
    to_z = [send(roots.at[b], roots.at[b], 10 + k, peer) for k, peer in enumerate(z_peers)]
    to_sides = [
        send(coef.at[own], coef.at[pl.ds(2 * LEAVES, LEAVES)], 17, left),
        send(coef.at[own], coef.at[pl.ds(0, LEAVES)], 18, right),
    ]
    ynodes[y] = pair[...]
    coef[own] = own_coef[...]
    loads[0].wait()
    shift = LEAVES - (b * CLUSTERS + c) * LEAVES

    def window_index(leaf):
        return jnp.minimum(jnp.maximum(leaf + shift, 0), 3 * LEAVES - 1)

    @pl.loop(0, LEAVES // GROUP)
    def _(step):
        found = []
        for inner in range(GROUP):
            n = step * GROUP + inner
            tn = target[n]
            high_sum = jnp.zeros((2 * SCEN, PANELS), f32)
            low_sum = jnp.zeros((SCEN, PANELS), f32)
            for slot in range(NEAR):
                m = window_index(near[n, slot])
                kernel = lax.rsqrt(dot(source[m], tn, 0, 0))
                kernel_high, kernel_low = halves(kernel)
                wm = weight[m]
                high_sum = high_sum + dot(wm, kernel_high, 1, 0)
                low_sum = low_sum + dot(wm[:SCEN], kernel_low, 1, 0)
            found.append((n, high_sum[:SCEN] + high_sum[SCEN:] + low_sum))
        for n, value in found:
            out[n] = value

        @pl.when(step == BARRIER_AT)
        def _():
            loads[1].wait()
            wait_for_all()
            for copy in to_y + to_sides:
                copy.start()

        @pl.when(step == Y_AT)
        def _():
            for copy in to_y:
                copy.wait()
            level = jnp.concatenate([ynodes[i] for i in range(NY)], axis=0)
            level = pair_up(up_tr, 1, rows(level, (0, 2, 4, 6)), rows(level, (1, 3, 5, 7)))
            for i in range(4):
                nodes2[i] = rows(level, (i,))
            level = pair_up(up_tr, 2, rows(level, (0, 2)), rows(level, (1, 3)))
            for i in range(2):
                nodes3[i] = rows(level, (i,))
            xnodes[x] = pair_up(up_tr, 3, rows(level, (0,)), rows(level, (1,)))
            for copy in to_x:
                copy.start()

        @pl.when(step == X_AT)
        def _():
            for copy in to_x:
                copy.wait()
            level = jnp.concatenate([xnodes[i] for i in range(NX)], axis=0)
            level = pair_up(up_tr, 4, rows(level, (0, 2)), rows(level, (1, 3)))
            for i in range(2):
                nodes5[i] = rows(level, (i,))
            roots[b] = pair_up(up_tr, 5, rows(level, (0,)), rows(level, (1,)))
            for copy in to_z:
                copy.start()

    for index in range(2, 5):
        loads[index].wait()
    for copy in to_sides:
        copy.wait()

    for n in range(LEAVES):
        total = jnp.zeros((SCEN, RANK), f32)
        for slot in range(FAR):
            total = total + dot3(coef[window_index(far[slot, n])], coupling[n, slot])
        local[n] = total
    for n in range(LEAVES):
        out[n] = out[n] + split_dot(halves(local[n]), halves(rowb[n]), 1, 0)

    siblings = (
        partner0[...],
        ynodes[flipped(y)],
        nodes2[flipped(y // 2)],
        nodes3[flipped(y // 4)],
        xnodes[flipped(x)],
        nodes5[flipped(x // 2)],
    )
    down = jnp.zeros((SCEN, RANK), f32)
    for level in range(LEVELS):
        down = down + dot3(siblings[level], way[level])
    for copy in to_z:
        copy.wait()
    for i in range(NZ - 1):
        down = down + dot3(roots[(b + 1 + i) % NZ], way[LEVELS + i])
    halved = halves(down)

    @pl.loop(0, LEAVES // 8)
    def _(step):
        for inner in range(8):
            n = step * 8 + inner
            out[n] = out[n] + split_dot(halved, (down_high[n], down_low[n]), 1, 0)


def on_device(charges, coords, areas, col, row, up, down, coupling, up_tr, down_tr, sib, branch, near, far):
    window = 3 * LEAVES
    hbm = pl.BlockSpec(memory_space=pltpu.HBM)
    node = (SCEN, RANK)
    square = (RANK, RANK)
    leaf_shape = (LEAVES, SCEN, PANELS)
    down_shape = (LEAVES, RANK, PANELS)
    made = (
        ((window, FEATURES, PANELS), bf16),
        ((window, 2 * SCEN, PANELS), bf16),
        ((LEAVES, FEATURES, PANELS), bf16),
        ((LEAVES,) + node, f32),
        (node, f32),
        (node, f32),
        ((LEVELS + NZ - 1,) + square, f32),
        (down_shape, bf16),
        (down_shape, bf16),
    )

    def vmem(*shape):
        return pltpu.VMEM(shape, f32)

    def params(collective_id, limit):
        return pltpu.CompilerParams(
            collective_id=collective_id, has_side_effects=True, vmem_limit_bytes=limit
        )

    passed = [pltpu.VMEM(shape, kind) for shape, kind in made]
    on_chip = pl.BlockSpec(memory_space=pltpu.VMEM)
    transfer = vmem(LEVELS, 2, *square)
    source, weight, target, coef, pair, partner, way, high, low = pl.pallas_call(
        exchange,
        out_shape=passed,
        in_specs=[hbm] * 11,
        out_specs=[on_chip] * 9,
        scratch_shapes=[
            vmem(window, SCEN, PANELS),
            vmem(3, window, PANELS),
            vmem(window, PANELS),
            vmem(LEAVES, RANK, PANELS),
            vmem(LEAVES, *square),
            transfer,
            vmem(LEAVES, *square),
            vmem(LEAVES, RANK, PANELS),
            transfer,
            transfer,
            vmem(NZ - 1, *square),
            vmem(*node),
            vmem(*node),
            pltpu.SemaphoreType.DMA((11,)),
            pltpu.SemaphoreType.DMA((7,)),
            pltpu.SemaphoreType.DMA((7,)),
        ],
        compiler_params=params(0, KERNEL_VMEM),
        name="exchange",
    )(
        charges,
        jnp.transpose(coords, (1, 0, 2)),
        areas,
        col,
        up,
        up_tr[0],
        down,
        row,
        down_tr[0],
        sib[0],
        branch[0],
    )
    source, weight, target, coef, pair, partner, way, high, low = (
        pltpu.with_memory_space_constraint(array, pltpu.VMEM)
        for array in (source, weight, target, coef, pair, partner, way, high, low)
    )
    return pl.pallas_call(
        near_field,
        out_shape=pltpu.VMEM(leaf_shape, f32),
        in_specs=[hbm] * 2 + [on_chip] * 6 + [hbm] * 3 + [on_chip] * 3,
        out_specs=on_chip,
        scratch_shapes=[
            pltpu.SMEM((LEAVES, NEAR), jnp.int32),
            pltpu.SMEM((FAR, LEAVES), jnp.int32),
            vmem(window, *node),
            vmem(LEAVES, FAR, *square),
            vmem(LEAVES, RANK, PANELS),
            transfer,
            vmem(LEAVES, *node),
            vmem(NY, *node),
            vmem(4, *node),
            vmem(2, *node),
            vmem(NX, *node),
            vmem(2, *node),
            vmem(NZ, *node),
            pltpu.SemaphoreType.DMA((5,)),
            pltpu.SemaphoreType.DMA((19,)),
            pltpu.SemaphoreType.DMA((19,)),
        ],
        compiler_params=params(1, KERNEL_VMEM),
        name="near_field",
    )(
        near,
        far.T,
        source,
        target,
        weight,
        coef,
        pair,
        partner,
        coupling,
        row,
        up_tr[0],
        way,
        high,
        low,
    )


def solution(mesh):
    leaf = ("branch", "cluster")

    def spec(axis, rank):
        return P(axis, *([None] * (rank - 1)))

    in_specs = (
        spec(leaf, 3),
        spec(leaf, 3),
        spec(leaf, 2),
        spec(leaf, 3),
        spec(leaf, 3),
        spec(leaf, 3),
        spec(leaf, 3),
        spec(leaf, 4),
        spec("branch", 5),
        spec("branch", 5),
        spec("branch", 5),
        spec("branch", 4),
        spec(leaf, 2),
        spec(leaf, 2),
    )
    return jax.shard_map(
        on_device, mesh=mesh, in_specs=in_specs, out_specs=spec(leaf, 3), check_vma=False
    )
```

```python
import functools
import math

import jax
import jax.numpy as jnp
from jax import lax
from jax.experimental import pallas as pl
from jax.experimental.pallas import tpu as pltpu
from jax.sharding import PartitionSpec as P

f32, bf16 = jnp.float32, jnp.bfloat16
MESH = pl.DeviceIdType.MESH
reg_square = 0.01
inv_four_pi = 0.25 / math.pi

LEAVES, SCEN, PANELS, RANK = 16, 16, 256, 64
NEAR, FAR, LEVELS = 16, 4, 6
NX, NY, NZ, CLUSTERS = 4, 8, 8, 64
FEATURES = 32
KERNEL_VMEM = 67043328 - (6 << 20)
GROUP = 2
BARRIER_AT, Y_AT, X_AT = 1, 3, 4
PAIRS = ((0, 0), (0, 1), (1, 0), (0, 2), (2, 0), (1, 1), (1, 2), (2, 1))


def dot(a, b, ca, cb):
    return lax.dot_general(a, b, (((ca,), (cb,)), ((), ())), preferred_element_type=f32)


def halves(x):
    high = x.astype(bf16)
    return high, (x - high.astype(f32)).astype(bf16)


def split_dot(a, b, ca, cb):
    rows = a[0].shape[1 - ca]
    both = dot(jnp.concatenate(a, axis=1 - ca), b[0], ca, cb)
    return both[:rows] + both[rows:] + dot(a[0], b[1], ca, cb)


def dot3(a, b, cb=1):
    return split_dot(halves(a), halves(b), 1, cb)


def features(x, y, z, is_source):
    row = lax.broadcasted_iota(jnp.int32, (FEATURES, PANELS), 0)
    dim = row % 3
    coord_row = row < 24
    x, y, z = (jnp.broadcast_to(value, (FEATURES, PANELS)) for value in (x, y, z))
    square = x * x + y * y + z * z
    value = jnp.where(dim == 0, x, jnp.where(dim == 1, y, z))
    pair = row // 3
    part = jnp.zeros_like(row)
    side = 0 if is_source else 1
    for index, parts in enumerate(PAIRS):
        if parts[side]:
            part = jnp.where(pair == index, parts[side], part)
    if is_source:
        value = jnp.where(coord_row, value, jnp.where(pair == 8, square, 1.0))
        part = jnp.where(pair == 8, dim, part)
    else:
        value = jnp.where(coord_row, -2.0 * value, jnp.where(pair == 8, 1.0, square + reg_square))
        part = jnp.where(pair == 9, dim, part)
    value = jnp.where(row < 30, value, 0.0)
    high = value.astype(bf16).astype(f32)
    rest = value - high
    middle = rest.astype(bf16).astype(f32)
    low = rest - middle
    return jnp.where(part == 0, high, jnp.where(part == 1, middle, low)).astype(bf16)


def place():
    b = lax.axis_index("branch")
    c = lax.axis_index("cluster")
    return b, c, c % 2, (c // 2) % NY, c // (2 * NY)


def remote(source_ref, target_ref, send_sem, recv_sem, index, peer):
    return pltpu.make_async_remote_copy(
        src_ref=source_ref,
        dst_ref=target_ref,
        send_sem=send_sem.at[index],
        recv_sem=recv_sem.at[index],
        device_id=peer,
        device_id_type=MESH,
    )


def greet(peers):
    barrier = pltpu.get_barrier_semaphore()
    for peer in peers:
        pl.semaphore_signal(barrier, inc=1, device_id=peer, device_id_type=MESH)
    return lambda: pl.semaphore_wait(barrier, len(peers))


def start_loads(pairs, sem):
    copies = [pltpu.make_async_copy(a, b, sem.at[i]) for i, (a, b) in enumerate(pairs)]
    for copy in copies:
        copy.start()
    return copies


def flipped(index):
    return index + 1 - 2 * (index % 2)


def pair_up(up_tr, level, left_child, right_child):
    return dot3(left_child, up_tr[level, 0]) + dot3(right_child, up_tr[level, 1])


def rows(nodes, picks):
    found = [nodes[SCEN * i : SCEN * i + SCEN] for i in picks]
    return found[0] if len(found) == 1 else jnp.concatenate(found, axis=0)


def exchange(
    charges_hbm,
    coords_hbm,
    areas_hbm,
    col_hbm,
    up_hbm,
    up_tr_hbm,
    down_hbm,
    row_hbm,
    down_tr_hbm,
    sibling_hbm,
    branch_hbm,
    source,
    weight,
    target,
    coef,
    pair,
    partner_out,
    way,
    down_high,
    down_low,
    charges,
    coords,
    areas,
    col,
    leaf_up,
    up_tr,
    leaf_down,
    rowb,
    down_tr,
    sibling,
    branch,
    node0,
    partner0,
    local_sem,
    send_sem,
    recv_sem,
):
    b, c, core, y, x = place()
    own = pl.ds(LEAVES, LEAVES)
    low_side, high_side = pl.ds(0, LEAVES), pl.ds(2 * LEAVES, LEAVES)
    left = (b, (c + CLUSTERS - 1) % CLUSTERS)
    right = (b, (c + 1) % CLUSTERS)
    partner = (b, flipped(c))
    wait_for_all = greet([left, right])

    loads = start_loads(
        (
            (coords_hbm, coords.at[:, own]),
            (areas_hbm, areas.at[own]),
            (charges_hbm, charges.at[own]),
            (col_hbm, col),
            (up_hbm, leaf_up),
            (up_tr_hbm, up_tr),
            (down_tr_hbm, down_tr),
            (sibling_hbm, sibling),
            (branch_hbm, branch),
            (down_hbm, leaf_down),
            (row_hbm, rowb),
        ),
        local_sem,
    )

    def send(source_ref, target_ref, index, peer):
        return remote(source_ref, target_ref, send_sem, recv_sem, index, peer)

    def sides(ref, index, lead):
        at = (lambda part: ref.at[:, part]) if lead else (lambda part: ref.at[part])
        return [send(at(own), at(high_side), index, left), send(at(own), at(low_side), index + 1, right)]

    coords_copies = sides(coords, 0, True)
    areas_copies = sides(areas, 2, False)
    charges_copies = sides(charges, 4, False)
    to_partner = send(node0, partner0, 6, partner)

    for index in range(3):
        loads[index].wait()
    wait_for_all()
    for copy in coords_copies + areas_copies + charges_copies:
        copy.start()

    loads[3].wait()

    @pl.loop(0, LEAVES // 8)
    def _(step):
        for inner in range(8):
            n = step * 8 + inner
            coef[n] = dot3(charges[LEAVES + n], col[n])

    loads[4].wait()

    def add_leaf(step, total):
        for inner in range(8):
            n = step * 8 + inner
            total = total + dot3(coef[n], leaf_up[n])
        return total

    node0[...] = lax.fori_loop(0, LEAVES // 8, add_leaf, jnp.zeros((SCEN, RANK), f32))
    to_partner.start()

    centres = []
    for i in range(3):
        mean = jnp.sum(coords[i, LEAVES : 2 * LEAVES], axis=0, keepdims=True)
        centres.append(jnp.sum(mean, axis=1, keepdims=True) * (1.0 / (LEAVES * PANELS)))

    def features_of(m, is_source):
        point = [coords[i, pl.ds(m, 1)] - centres[i] for i in range(3)]
        return features(*point, is_source)

    def weigh(m):
        high, low = halves(charges[m] * (areas[pl.ds(m, 1)] * inv_four_pi))
        weight[m, 0:SCEN] = high
        weight[m, SCEN : 2 * SCEN] = low

    @pl.loop(0, LEAVES // 2)
    def _(step):
        for inner in range(2):
            n = step * 2 + inner
            source[LEAVES + n] = features_of(LEAVES + n, True)
            target[n] = features_of(LEAVES + n, False)
            weigh(LEAVES + n)

    loads[5].wait()
    to_partner.wait()
    mine, other = node0[...], partner0[...]
    even = core == 0
    pair[...] = pair_up(up_tr, 0, jnp.where(even, mine, other), jnp.where(even, other, mine))
    partner_out[...] = other

    for index in range(6, 11):
        loads[index].wait()
    side = (core, y % 2, (y // 2) % 2, y // 4, x % 2, x // 2)
    way[0] = sibling[0, side[0]]
    path = down_tr[0, side[0]]
    for level in range(1, LEVELS):
        way[level] = dot3(path, sibling[level, side[level]], 0)
        path = dot3(path, down_tr[level, side[level]], 0)
    path_halves = halves(path)
    for i in range(NZ - 1):
        way[LEVELS + i] = split_dot(path_halves, halves(branch[i]), 1, 0)

    @pl.loop(0, LEAVES // 8)
    def _(step):
        for inner in range(8):
            n = step * 8 + inner
            product = split_dot(halves(leaf_down[n]), halves(rowb[n]), 0, 0)
            down_high[n], down_low[n] = halves(product)


    for copy in coords_copies:
        copy.wait()

    @pl.loop(0, LEAVES // 2)
    def _(step):
        for inner in range(2):
            n = step * 2 + inner
            source[n] = features_of(n, True)
            source[2 * LEAVES + n] = features_of(2 * LEAVES + n, True)

    for copy in areas_copies + charges_copies:
        copy.wait()

    @pl.loop(0, LEAVES // 4)
    def _(step):
        for inner in range(4):
            n = step * 4 + inner
            weigh(n)
            weigh(2 * LEAVES + n)


def near_field(
    near_hbm,
    far_hbm,
    source,
    target,
    weight,
    own_coef,
    pair,
    partner0,
    coupling_hbm,
    row_hbm,
    up_tr_hbm,
    way,
    down_high,
    down_low,
    out,
    near,
    far,
    coef,
    coupling,
    rowb,
    up_tr,
    local,
    ynodes,
    nodes2,
    nodes3,
    xnodes,
    nodes5,
    roots,
    local_sem,
    send_sem,
    recv_sem,
):
    b, c, core, y, x = place()
    y_peers = [(b, (x * NY + (y + k) % NY) * 2 + core) for k in range(1, NY)]
    x_peers = [(b, (((x + k) % NX) * NY + y) * 2 + core) for k in range(1, NX)]
    z_peers = [((b + k) % NZ, c) for k in range(1, NZ)]
    left = (b, (c + CLUSTERS - 1) % CLUSTERS)
    right = (b, (c + 1) % CLUSTERS)
    own = pl.ds(LEAVES, LEAVES)
    wait_for_all = greet([left, right] + y_peers + x_peers + z_peers)
    loads = start_loads(
        (
            (near_hbm, near),
            (up_tr_hbm, up_tr),
            (far_hbm, far),
            (coupling_hbm, coupling),
            (row_hbm, rowb),
        ),
        local_sem,
    )

    def send(source_ref, target_ref, index, peer):
        return remote(source_ref, target_ref, send_sem, recv_sem, index, peer)

    to_y = [send(ynodes.at[y], ynodes.at[y], k, peer) for k, peer in enumerate(y_peers)]
    to_x = [send(xnodes.at[x], xnodes.at[x], 7 + k, peer) for k, peer in enumerate(x_peers)]
    to_z = [send(roots.at[b], roots.at[b], 10 + k, peer) for k, peer in enumerate(z_peers)]
    to_sides = [
        send(coef.at[own], coef.at[pl.ds(2 * LEAVES, LEAVES)], 17, left),
        send(coef.at[own], coef.at[pl.ds(0, LEAVES)], 18, right),
    ]
    ynodes[y] = pair[...]
    coef[own] = own_coef[...]
    loads[0].wait()
    shift = LEAVES - (b * CLUSTERS + c) * LEAVES

    def window_index(leaf):
        return jnp.minimum(jnp.maximum(leaf + shift, 0), 3 * LEAVES - 1)

    @pl.loop(0, LEAVES // GROUP)
    def _(step):
        found = []
        for inner in range(GROUP):
            n = step * GROUP + inner
            tn = target[n]
            high_sum = jnp.zeros((2 * SCEN, PANELS), f32)
            low_sum = jnp.zeros((SCEN, PANELS), f32)
            for slot in range(NEAR):
                m = window_index(near[n, slot])
                kernel = lax.rsqrt(dot(source[m], tn, 0, 0))
                kernel_high, kernel_low = halves(kernel)
                wm = weight[m]
                high_sum = high_sum + dot(wm, kernel_high, 1, 0)
                low_sum = low_sum + dot(wm[:SCEN], kernel_low, 1, 0)
            found.append((n, high_sum[:SCEN] + high_sum[SCEN:] + low_sum))
        for n, value in found:
            out[n] = value

        @pl.when(step == BARRIER_AT)
        def _():
            loads[1].wait()
            wait_for_all()
            for copy in to_y + to_sides:
                copy.start()

        @pl.when(step == Y_AT)
        def _():
            for copy in to_y:
                copy.wait()
            level = jnp.concatenate([ynodes[i] for i in range(NY)], axis=0)
            level = pair_up(up_tr, 1, rows(level, (0, 2, 4, 6)), rows(level, (1, 3, 5, 7)))
            for i in range(4):
                nodes2[i] = rows(level, (i,))
            level = pair_up(up_tr, 2, rows(level, (0, 2)), rows(level, (1, 3)))
            for i in range(2):
                nodes3[i] = rows(level, (i,))
            xnodes[x] = pair_up(up_tr, 3, rows(level, (0,)), rows(level, (1,)))
            for copy in to_x:
                copy.start()

        @pl.when(step == X_AT)
        def _():
            for copy in to_x:
                copy.wait()
            level = jnp.concatenate([xnodes[i] for i in range(NX)], axis=0)
            level = pair_up(up_tr, 4, rows(level, (0, 2)), rows(level, (1, 3)))
            for i in range(2):
                nodes5[i] = rows(level, (i,))
            roots[b] = pair_up(up_tr, 5, rows(level, (0,)), rows(level, (1,)))
            for copy in to_z:
                copy.start()

    for index in range(2, 5):
        loads[index].wait()
    for copy in to_sides:
        copy.wait()

    for n in range(LEAVES):
        total = jnp.zeros((SCEN, RANK), f32)
        for slot in range(FAR):
            total = total + dot3(coef[window_index(far[slot, n])], coupling[n, slot])
        local[n] = total
    for n in range(LEAVES):
        out[n] = out[n] + split_dot(halves(local[n]), halves(rowb[n]), 1, 0)

    siblings = (
        partner0[...],
        ynodes[flipped(y)],
        nodes2[flipped(y // 2)],
        nodes3[flipped(y // 4)],
        xnodes[flipped(x)],
        nodes5[flipped(x // 2)],
    )
    down = jnp.zeros((SCEN, RANK), f32)
    for level in range(LEVELS):
        down = down + dot3(siblings[level], way[level])
    for copy in to_z:
        copy.wait()
    for i in range(NZ - 1):
        down = down + dot3(roots[(b + 1 + i) % NZ], way[LEVELS + i])
    halved = halves(down)

    @pl.loop(0, LEAVES // 8)
    def _(step):
        for inner in range(8):
            n = step * 8 + inner
            out[n] = out[n] + split_dot(halved, (down_high[n], down_low[n]), 1, 0)


def on_device(charges, coords, areas, col, row, up, down, coupling, up_tr, down_tr, sib, branch, near, far):
    window = 3 * LEAVES
    hbm = pl.BlockSpec(memory_space=pltpu.HBM)
    node = (SCEN, RANK)
    square = (RANK, RANK)
    leaf_shape = (LEAVES, SCEN, PANELS)
    down_shape = (LEAVES, RANK, PANELS)
    made = (
        ((window, FEATURES, PANELS), bf16),
        ((window, 2 * SCEN, PANELS), bf16),
        ((LEAVES, FEATURES, PANELS), bf16),
        ((LEAVES,) + node, f32),
        (node, f32),
        (node, f32),
        ((LEVELS + NZ - 1,) + square, f32),
        (down_shape, bf16),
        (down_shape, bf16),
    )

    def vmem(*shape):
        return pltpu.VMEM(shape, f32)

    def params(collective_id, limit):
        return pltpu.CompilerParams(
            collective_id=collective_id, has_side_effects=True, vmem_limit_bytes=limit
        )

    passed = [pltpu.VMEM(shape, kind) for shape, kind in made]
    on_chip = pl.BlockSpec(memory_space=pltpu.VMEM)
    transfer = vmem(LEVELS, 2, *square)
    source, weight, target, coef, pair, partner, way, high, low = pl.pallas_call(
        exchange,
        out_shape=passed,
        in_specs=[hbm] * 11,
        out_specs=[on_chip] * 9,
        scratch_shapes=[
            vmem(window, SCEN, PANELS),
            vmem(3, window, PANELS),
            vmem(window, PANELS),
            vmem(LEAVES, RANK, PANELS),
            vmem(LEAVES, *square),
            transfer,
            vmem(LEAVES, *square),
            vmem(LEAVES, RANK, PANELS),
            transfer,
            transfer,
            vmem(NZ - 1, *square),
            vmem(*node),
            vmem(*node),
            pltpu.SemaphoreType.DMA((11,)),
            pltpu.SemaphoreType.DMA((7,)),
            pltpu.SemaphoreType.DMA((7,)),
        ],
        compiler_params=params(0, KERNEL_VMEM),
        name="exchange",
    )(
        charges,
        jnp.transpose(coords, (1, 0, 2)),
        areas,
        col,
        up,
        up_tr[0],
        down,
        row,
        down_tr[0],
        sib[0],
        branch[0],
    )
    source, weight, target, coef, pair, partner, way, high, low = (
        pltpu.with_memory_space_constraint(array, pltpu.VMEM)
        for array in (source, weight, target, coef, pair, partner, way, high, low)
    )
    return pl.pallas_call(
        near_field,
        out_shape=pltpu.VMEM(leaf_shape, f32),
        in_specs=[hbm] * 2 + [on_chip] * 6 + [hbm] * 3 + [on_chip] * 3,
        out_specs=on_chip,
        scratch_shapes=[
            pltpu.SMEM((LEAVES, NEAR), jnp.int32),
            pltpu.SMEM((FAR, LEAVES), jnp.int32),
            vmem(window, *node),
            vmem(LEAVES, FAR, *square),
            vmem(LEAVES, RANK, PANELS),
            transfer,
            vmem(LEAVES, *node),
            vmem(NY, *node),
            vmem(4, *node),
            vmem(2, *node),
            vmem(NX, *node),
            vmem(2, *node),
            vmem(NZ, *node),
            pltpu.SemaphoreType.DMA((5,)),
            pltpu.SemaphoreType.DMA((19,)),
            pltpu.SemaphoreType.DMA((19,)),
        ],
        compiler_params=params(1, KERNEL_VMEM),
        name="near_field",
    )(
        near,
        far.T,
        source,
        target,
        weight,
        coef,
        pair,
        partner,
        coupling,
        row,
        up_tr[0],
        way,
        high,
        low,
    )


def solution(mesh):
    leaf = ("branch", "cluster")

    def spec(axis, rank):
        return P(axis, *([None] * (rank - 1)))

    in_specs = (
        spec(leaf, 3),
        spec(leaf, 3),
        spec(leaf, 2),
        spec(leaf, 3),
        spec(leaf, 3),
        spec(leaf, 3),
        spec(leaf, 3),
        spec(leaf, 4),
        spec("branch", 5),
        spec("branch", 5),
        spec("branch", 5),
        spec("branch", 4),
        spec(leaf, 2),
        spec(leaf, 2),
    )
    return jax.shard_map(
        on_device, mesh=mesh, in_specs=in_specs, out_specs=spec(leaf, 3), check_vma=False
    )
```
